256 devices in a mesh: dp: 64 (over z, x, core), mp: 4 (over y).
Axes of the slice: x: 4, y: 4, z: 8, core: 2. Of those that a mesh axis runs over, the one named last changes fastest.
Arguments:
- tokens: bfloat16 [32768, 8192], P('dp', 'mp'), may hold values from -6 to 6
- base_weight: bfloat16 [8192, 1024], P('mp'), may hold values from -0.0625 to 0.0625
- adapter_down: bfloat16 [256, 32, 8192], P('dp', None, 'mp'), may hold values from -0.0625 to 0.0625
- adapter_up: bfloat16 [256, 32, 1024], P('dp', None, 'mp'), may hold values from -1 to 1
- block_adapter: int32 [1024], P('dp'), may hold values from 0 to 255, as said below
- cotangent: bfloat16 [32768, 1024], P('dp', 'mp'), may hold values from -6 to 6
Outputs:
- output: bfloat16 [32768, 1024], P('dp', 'mp')
- input_grad: bfloat16 [32768, 8192], P('dp', 'mp')
- down_grad: float32 [256, 32, 8192], P('dp', None, 'mp')
- up_grad: float32 [256, 32, 1024], P('dp', None, 'mp')
The draws below stay inside these ranges and needn't reach their ends.
Inputs may be any that keep to these rules, and one draw needn't show every extreme that they name: `block_adapter`: adapter a is owned by index a // 4 of dp; the 16 blocks of one index of dp name adapters of 16 different owners.
All inputs are finite; a program needn't handle non-finite values.
Results may differ from the reference program's by a relative error of at most 0.0045.
Values may be sent and summed in bfloat16 or wider, within the bound.
No kernel may reach another device: no remote copies, remote signals or barrier semaphores. Data moves between devices by JAX's collectives and lax.ppermute only.
A program may use at most 128 MiB of HBM per device.

```python
import jax
import jax.numpy as jnp
from jax import lax

D = 8192
KV = 1024
R = 32
BLOCK_TOKENS = 32
BLOCKS = 16
ADP_DEV = 4
ADAPTERS = 256
TOKENS = 32768
N_DP = 64


def draw_block_adapter(key, part):
    key_order = jax.random.fold_in(key, 11)
    key_score = jax.random.fold_in(key, 12)
    key_local = jax.random.fold_in(key, 13)
    order = jax.random.permutation(key_order, N_DP).astype(jnp.int32)
    weights = (1048576 // (order + 1)).astype(jnp.int32)
    raw = jax.random.randint(key_score, (N_DP, N_DP), 0, 1048576, dtype=jnp.int32)
    scores = raw % weights[None, :] * N_DP + jnp.arange(N_DP, dtype=jnp.int32)[None, :]
    picked = lax.top_k(scores, BLOCKS)[1].astype(jnp.int32)
    local = jax.random.randint(key_local, (N_DP, BLOCKS), 0, ADP_DEV, dtype=jnp.int32)
    return (picked * ADP_DEV + local).reshape(N_DP * BLOCKS)


def block_scale(own_key, extent, shards, low, largest):
    gain = 1.0
    for position, parts in shards:
        heights = jax.random.uniform(jax.random.fold_in(jax.random.fold_in(own_key, 6), position), (parts,), jnp.float32, low / len(shards), largest / len(shards))
        gain = gain * jnp.repeat(jnp.exp(heights), extent[position] // parts).reshape((-1,) + (1,) * (len(extent) - 1 - position))
    return gain


def bell_draw(own_key, extent, scale, bound, split=(), kind=jnp.bfloat16):
    array = scale * jax.random.normal(own_key, extent, jnp.float32)
    if split:
        array = array * block_scale(own_key, extent, split, -0.22, 0.18)
    return jnp.clip(array, -bound, bound).astype(kind)


def setup_inputs(seed: int = 0) -> dict:
    key_list = jax.random.split(jax.random.key(seed), 7)
    tokens = bell_draw(key_list[0], (TOKENS, D), 1.0, 6.0, ((0, 64), (1, 4)))
    base_weight = bell_draw(key_list[1], (D, KV), D ** -0.5, 0.0625, ((0, 4),))
    adapter_down = bell_draw(key_list[2], (ADAPTERS, R, D), D ** -0.5, 0.0625, ((0, 64), (2, 4)))
    adapter_up = bell_draw(key_list[3], (ADAPTERS, R, KV), R ** -0.5, 1.0, ((0, 64), (2, 4)))
    block_adapter = draw_block_adapter(jax.random.fold_in(key_list[6], 71), 0)
    cotangent = bell_draw(key_list[5], (TOKENS, KV), 1.0, 6.0, ((0, 64), (1, 4)))
    return dict(tokens=tokens, base_weight=base_weight, adapter_down=adapter_down, adapter_up=adapter_up, block_adapter=block_adapter, cotangent=cotangent)


adapter_scale = 2.0


def reference(tokens, base_weight, adapter_down, adapter_up, block_adapter, cotangent):
    count = tokens.shape[0] // BLOCK_TOKENS
    token_blocks = tokens.reshape(count, BLOCK_TOKENS, D)
    cot_blocks = cotangent.reshape(count, BLOCK_TOKENS, KV)

    def per_block(totals, pieces):
        down_total, up_total = totals
        token_block, cotangent_rows, which = pieces
        down = lax.dynamic_index_in_dim(adapter_down, which, 0, keepdims=False)
        upper_bound = lax.dynamic_index_in_dim(adapter_up, which, 0, keepdims=False)
        adapter_rank = jnp.dot(token_block, down.T, preferred_element_type=jnp.float32).astype(jnp.bfloat16)
        frozen_output = jnp.dot(token_block, base_weight, preferred_element_type=jnp.float32)
        adapted_output = jnp.dot(adapter_rank, upper_bound, preferred_element_type=jnp.float32)
        final_output = (frozen_output + adapter_scale * adapted_output).astype(jnp.bfloat16)
        rank_gradient = (adapter_scale * jnp.dot(cotangent_rows, upper_bound.T, preferred_element_type=jnp.float32)).astype(jnp.bfloat16)
        input_grad = (jnp.dot(cotangent_rows, base_weight.T, preferred_element_type=jnp.float32)
                      + jnp.dot(rank_gradient, down, preferred_element_type=jnp.float32)).astype(jnp.bfloat16)
        down_term = jnp.dot(rank_gradient.T, token_block, preferred_element_type=jnp.float32) / BLOCK_TOKENS
        up_product = adapter_scale * jnp.dot(adapter_rank.T, cotangent_rows, preferred_element_type=jnp.float32) / BLOCK_TOKENS
        down_total = down_total.at[which].add(down_term)
        up_total = up_total.at[which].add(up_product)
        return (down_total, up_total), (final_output, input_grad)

    start = (jnp.zeros((ADAPTERS, R, D), jnp.float32), jnp.zeros((ADAPTERS, R, KV), jnp.float32))
    totals, outputs = lax.scan(per_block, start, (token_blocks, cot_blocks, block_adapter.astype(jnp.int32)))
    output = outputs[0].reshape(count * BLOCK_TOKENS, KV)
    input_grad = outputs[1].reshape(count * BLOCK_TOKENS, D)
    return (output, input_grad, totals[0], totals[1])
```

```python
import jax
import jax.numpy as jnp
from jax import lax
from jax.sharding import Mesh, PartitionSpec as P

adapter_scale = 2.0
PLANE = 8


def shards(tokens, base_weight, adapter_down, adapter_up, block_adapter, cotangent):
    f32, bf = jnp.float32, jnp.bfloat16
    blocks = block_adapter.shape[0]
    owned = adapter_down.shape[0]
    width_local = tokens.shape[1]
    local_columns = cotangent.shape[1]
    dp = ("z", "g")
    planes = lax.axis_size("z")
    plane = lax.axis_size("g")
    adapters = planes * plane * owned
    narrow = width_local // plane
    block_len = tokens.shape[0] // blocks

    ids = block_adapter
    ids_plane = lax.all_gather(ids, "g", axis=0, tiled=True)

    up_all = lax.all_gather(adapter_up, dp, axis=0, tiled=True)
    up_blk = jnp.take(up_all, ids, axis=0)
    cot_blk = cotangent.reshape(blocks, block_len, local_columns)
    local_term = jnp.einsum("btk,brk->btr", cot_blk, up_blk, preferred_element_type=f32)
    rank_gradient = (adapter_scale * lax.psum(local_term, "mp")).astype(bf)
    rg_plane = lax.all_gather(rank_gradient, "g", axis=0, tiled=True)

    tok_n = lax.all_to_all(tokens, "g", split_axis=1, concat_axis=0, tiled=True)
    tok_nb = tok_n.reshape(plane * blocks, block_len, narrow)
    down_n = lax.all_to_all(adapter_down, "g", split_axis=2, concat_axis=0, tiled=True)
    table = lax.all_gather(down_n, "z", axis=0, tiled=True)
    down_nb = jnp.take(table, ids_plane, axis=0)

    down_terms = jnp.einsum("btr,btd->brd", rg_plane, tok_nb, preferred_element_type=f32) / block_len
    route = (jnp.arange(adapters, dtype=jnp.int32)[:, None] == ids_plane[None, :]).astype(f32)
    grad_table = jnp.einsum("ab,brd->ard", route, down_terms, precision=lax.Precision.HIGHEST)
    grad_n = lax.psum_scatter(grad_table.astype(bf), "z", scatter_dimension=0, tiled=True)
    down_grad = lax.all_to_all(grad_n, "g", split_axis=0, concat_axis=2, tiled=True).astype(f32)

    through_n = jnp.einsum("btr,brd->btd", rg_plane, down_nb, preferred_element_type=f32)
    through = lax.all_to_all(
        through_n.reshape(-1, narrow).astype(bf), "g", split_axis=0, concat_axis=1, tiled=True
    )

    rank_part = jnp.einsum("btd,brd->btr", tok_nb, down_nb, preferred_element_type=f32)
    rank_parts = lax.all_to_all(
        rank_part.reshape(plane, blocks, block_len, -1), "g", split_axis=0, concat_axis=0, tiled=True
    )
    rank_vals = lax.psum(jnp.sum(rank_parts, axis=0), "mp").astype(bf)

    base_part = jnp.dot(tokens, base_weight, preferred_element_type=f32)
    frozen_columns = lax.psum_scatter(base_part, "mp", scatter_dimension=1, tiled=True)
    adapted_output = jnp.einsum("btr,brk->btk", rank_vals, up_blk, preferred_element_type=f32)
    output = (frozen_columns + adapter_scale * adapted_output.reshape(-1, local_columns)).astype(bf)

    cot_full = lax.all_gather(cotangent, "mp", axis=1, tiled=True)
    through_base = jnp.dot(cot_full, base_weight.T, preferred_element_type=f32)
    input_grad = (through_base + through.astype(f32)).astype(bf)

    up_terms = (
        adapter_scale
        * jnp.einsum("btr,btk->brk", rank_vals, cot_blk, preferred_element_type=f32)
        / block_len
    )
    route_up = (jnp.arange(adapters, dtype=jnp.int32)[:, None] == ids[None, :]).astype(f32)
    up_table = jnp.einsum("ab,brk->ark", route_up, up_terms, precision=lax.Precision.HIGHEST)
    up_grad = lax.psum_scatter(up_table.astype(bf), dp, scatter_dimension=0, tiled=True).astype(f32)
    return (output, input_grad, down_grad, up_grad)


def solution(mesh):
    fine = Mesh(mesh.devices.reshape(-1, PLANE, mesh.devices.shape[1]), ("z", "g", "mp"))
    dp = ("z", "g")
    return jax.shard_map(
        shards,
        mesh=fine,
        in_specs=(
            P(dp, "mp"),
            P("mp", None),
            P(dp, None, "mp"),
            P(dp, None, "mp"),
            P(dp),
            P(dp, "mp"),
        ),
        out_specs=(P(dp, "mp"), P(dp, "mp"), P(dp, None, "mp"), P(dp, None, "mp")),
        check_vma=False,
    )
```

```python
import functools

import jax
import jax.numpy as jnp
from jax import lax
from jax.experimental import pallas as pl
from jax.experimental.pallas import tpu as pltpu
from jax.sharding import Mesh, PartitionSpec as P

adapter_scale = 2.0
PLANE = 8
QUAD = 4
f32, bf = jnp.float32, jnp.bfloat16

SMEM = functools.partial(pl.BlockSpec, memory_space=pltpu.SMEM)
VMEM = functools.partial(pl.BlockSpec, memory_space=pltpu.VMEM)


def diagonal(length, rank):
    rows = lax.broadcasted_iota(jnp.int32, (QUAD * length, QUAD * rank), 0) // length
    cols = lax.broadcasted_iota(jnp.int32, (QUAD * length, QUAD * rank), 1) // rank
    return rows == cols


def fold(product, mask, length):
    kept = jnp.where(mask, product, 0.0)
    total = kept[:length]
    for i in range(1, QUAD):
        total = total + kept[i * length : (i + 1) * length]
    return total


def spread(quad, mask):
    wide = jnp.concatenate([quad] * QUAD, axis=0)
    return jnp.where(mask, wide, jnp.zeros_like(wide))


def dot_nt(a, b):
    return lax.dot_general(a, b, (((1,), (1,)), ((), ())), preferred_element_type=f32)


def dot_nn(a, b):
    return lax.dot_general(a, b, (((1,), (0,)), ((), ())), preferred_element_type=f32)


def dot_tn(a, b):
    return lax.dot_general(a, b, (((0,), (0,)), ((), ())), preferred_element_type=f32)


def select_up(ids_all, me, pieces, owned, planes, plane):
    rank, cols = pieces[0].shape[1:]
    count = ids_all.shape[0]
    blocks = count // plane

    def kernel(ids_ref, me_ref, *refs):
        parts, out_ref, stack = refs[:planes], refs[planes], refs[planes + 1]
        my_z, my_g = me_ref[0], me_ref[1]
        for k in range(planes):
            stack[(my_z - k + planes) % planes] = parts[k][...]

        def step(b, carry):
            owner = ids_ref[b] // owned
            local = ids_ref[b] % owned

            @pl.when(owner % plane == my_g)
            def _():
                out_ref[b // blocks, owner // plane] = stack[owner // plane, local]

            return carry

        lax.fori_loop(0, count, step, 0)

    return pl.pallas_call(
        kernel,
        in_specs=[SMEM(), SMEM()] + [VMEM()] * planes,
        out_specs=VMEM(),
        out_shape=jax.ShapeDtypeStruct((plane, planes, rank, cols), bf),
        scratch_shapes=[pltpu.VMEM((planes, owned, rank, cols), bf)],
        name="select_up",
    )(ids_all, me, *pieces)


def up_rows(ids_ref, slots_ref, q, owned, plane):
    rows = []
    for i in range(QUAD):
        owner = ids_ref[q * QUAD + i] // owned
        rows.append(slots_ref[owner % plane, owner // plane])
    return jnp.concatenate(rows, axis=0)


def rank_grad_part(ids, slots, cot, owned):
    plane, planes, rank, cols = slots.shape
    blocks = ids.shape[0]
    length = cot.shape[0] // blocks
    quads = blocks // QUAD
    span = QUAD * length

    def kernel(ids_ref, slots_ref, cot_ref, out_ref):
        mask = diagonal(length, rank)
        for q in range(quads):
            up = up_rows(ids_ref, slots_ref, q, owned, plane)
            out_ref[q] = fold(dot_nt(cot_ref[q * span : (q + 1) * span, :], up), mask, length)

    return pl.pallas_call(
        kernel,
        in_specs=[SMEM(), VMEM(), VMEM()],
        out_specs=VMEM(),
        out_shape=jax.ShapeDtypeStruct((quads, length, QUAD * rank), f32),
        name="rank_grad_part",
    )(ids, slots, cot)


def down_terms(ids_all, me, rg, tok, adapters, rank):
    plane = len(rg)
    quads, length = rg[0].shape[:2]
    span = QUAD * length
    blocks = quads * QUAD
    narrow = tok.shape[2]

    def kernel(ids_ref, me_ref, *refs):
        rgs, tok_ref, out_ref, acc = refs[:plane], refs[plane], refs[plane + 1], refs[plane + 2]
        mask = diagonal(length, rank)

        def clear(c, carry):
            acc[pl.ds(c * 8, 8)] = jnp.zeros((8, rank, narrow), f32)
            return carry

        lax.fori_loop(0, adapters // 8, clear, 0)
        for k in range(plane):
            src = (me_ref[1] - k + plane) % plane
            for q in range(quads):
                wide = spread(rgs[k][q], mask)
                got = dot_tn(wide, tok_ref[src, q * span : (q + 1) * span, :]) * (1.0 / length)
                for i in range(QUAD):
                    a = ids_ref[src * blocks + q * QUAD + i]
                    acc[a] = acc[a] + got[i * rank : (i + 1) * rank]

        def finish(c, carry):
            out_ref[pl.ds(c * 8, 8)] = acc[pl.ds(c * 8, 8)].astype(bf)
            return carry

        lax.fori_loop(0, adapters // 8, finish, 0)

    return pl.pallas_call(
        kernel,
        in_specs=[SMEM(), SMEM()] + [VMEM()] * (plane + 1),
        out_specs=VMEM(),
        out_shape=jax.ShapeDtypeStruct((adapters, rank, narrow), bf),
        scratch_shapes=[pltpu.VMEM((adapters, rank, narrow), f32)],
        name="down_terms",
    )(ids_all, me, *rg, tok)


def table_rows(ids_ref, table_ref, first):
    return jnp.concatenate([table_ref[ids_ref[first + i]] for i in range(QUAD)], axis=0)


def rank_part(ids_all, table, tok):
    plane, tokens, narrow = tok.shape
    rank = table.shape[1]
    blocks = ids_all.shape[0] // plane
    length = tokens // blocks
    quads = blocks // QUAD
    span = QUAD * length

    def kernel(ids_ref, table_ref, tok_ref, out_ref):
        mask = diagonal(length, rank)

        def step(s, carry):
            for q in range(quads):
                down = table_rows(ids_ref, table_ref, s * blocks + q * QUAD)
                got = dot_nt(tok_ref[s, q * span : (q + 1) * span, :], down)
                out_ref[s, q] = fold(got, mask, length)
            return carry

        lax.fori_loop(0, plane, step, 0)

    return pl.pallas_call(
        kernel,
        in_specs=[SMEM(), VMEM(), VMEM()],
        out_specs=VMEM(),
        out_shape=jax.ShapeDtypeStruct((plane, quads, length, QUAD * rank), f32),
        name="rank_part",
    )(ids_all, table, tok)


def through_down(ids_all, me, table, rg):
    plane = len(rg)
    quads, length = rg[0].shape[:2]
    rank, narrow = table.shape[1:]
    span = QUAD * length
    blocks = quads * QUAD

    def kernel(ids_ref, me_ref, table_ref, *refs):
        rgs, out_ref = refs[:plane], refs[plane]
        mask = diagonal(length, rank)
        for k in range(plane):
            src = (me_ref[1] - k + plane) % plane
            for q in range(quads):
                down = table_rows(ids_ref, table_ref, src * blocks + q * QUAD)
                got = dot_nn(spread(rgs[k][q], mask), down)
                out_ref[src, q * span : (q + 1) * span, :] = got.astype(bf)

    return pl.pallas_call(
        kernel,
        in_specs=[SMEM(), SMEM(), VMEM()] + [VMEM()] * plane,
        out_specs=VMEM(),
        out_shape=jax.ShapeDtypeStruct((plane, quads * span, narrow), bf),
        name="through_down",
    )(ids_all, me, table, *rg)


def output_and_up(ids, ranks, slots, cot, base, owned):
    plane, planes, rank, cols = slots.shape
    quads, length = ranks.shape[:2]
    span = QUAD * length

    def kernel(ids_ref, rank_ref, slots_ref, cot_ref, base_ref, out_ref, send_ref):
        mask = diagonal(length, rank)
        for q in range(quads):
            wide = spread(rank_ref[q], mask)
            up = up_rows(ids_ref, slots_ref, q, owned, plane)
            rows = slice(q * span, (q + 1) * span)
            out_ref[rows, :] = (base_ref[rows, :] + adapter_scale * dot_nn(wide, up)).astype(bf)
            got = (dot_tn(wide, cot_ref[rows, :]) * (adapter_scale / length)).astype(bf)
            for i in range(QUAD):
                owner = ids_ref[q * QUAD + i] // owned
                send_ref[owner % plane, owner // plane] = got[i * rank : (i + 1) * rank]

    return pl.pallas_call(
        kernel,
        in_specs=[SMEM()] + [VMEM()] * 4,
        out_specs=(VMEM(), VMEM()),
        out_shape=(
            jax.ShapeDtypeStruct(cot.shape, bf),
            jax.ShapeDtypeStruct(slots.shape, bf),
        ),
        name="output_and_up",
    )(ids, ranks, slots, cot, base)


def gather_up(ids_all, me, got, owned):
    plane, planes, rank, cols = got.shape
    count = ids_all.shape[0]
    blocks = count // plane

    def kernel(ids_ref, me_ref, got_ref, *refs):
        outs, acc = refs[:planes], refs[planes]
        my_z, my_g = me_ref[0], me_ref[1]
        acc[...] = jnp.zeros(acc.shape, f32)

        def step(b, carry):
            owner = ids_ref[b] // owned
            local = ids_ref[b] % owned

            @pl.when(owner % plane == my_g)
            def _():
                z = owner // plane
                acc[z, local] = acc[z, local] + got_ref[b // blocks, z].astype(f32)

            return carry

        lax.fori_loop(0, count, step, 0)
        for k in range(planes):
            outs[k][...] = acc[(my_z + k) % planes].astype(outs[k].dtype)

    chunk = (owned, rank, cols)
    return pl.pallas_call(
        kernel,
        in_specs=[SMEM(), SMEM(), VMEM()],
        out_specs=tuple([VMEM()] * planes),
        out_shape=tuple(jax.ShapeDtypeStruct(chunk, bf if k else f32) for k in range(planes)),
        scratch_shapes=[pltpu.VMEM((planes,) + chunk, f32)],
        name="gather_up",
    )(ids_all, me, got)


def input_gradient(cot_all, weight, through):
    parts, tokens, cols = cot_all.shape
    plane, _, narrow = through.shape

    def kernel(cot_ref, w_ref, thr_ref, out_ref):
        total = thr_ref[0].astype(f32)
        for j in range(parts):
            total = total + dot_nt(cot_ref[j], w_ref[:, j * cols : (j + 1) * cols])
        out_ref[...] = total.astype(bf)

    return pl.pallas_call(
        kernel,
        grid=(plane,),
        in_specs=[
            pl.BlockSpec((parts, tokens, cols), lambda s: (0, 0, 0)),
            pl.BlockSpec((narrow, parts * cols), lambda s: (s, 0)),
            pl.BlockSpec((1, tokens, narrow), lambda s: (s, 0, 0)),
        ],
        out_specs=pl.BlockSpec((tokens, narrow), lambda s: (0, s)),
        out_shape=jax.ShapeDtypeStruct((tokens, plane * narrow), bf),
        name="input_gradient",
    )(cot_all, weight, through)


def shift(x, axis, size, k):
    return lax.ppermute(x, axis, [(i, (i + k) % size) for i in range(size)])


def shards(tokens, base_weight, adapter_down, adapter_up, block_adapter, cotangent):
    blocks = block_adapter.shape[0]
    owned, rank, width_local = adapter_down.shape
    tokens_local, local_columns = cotangent.shape
    planes, plane, parts = lax.axis_size("z"), lax.axis_size("g"), lax.axis_size("mp")
    my_mp = lax.axis_index("mp")
    me = jnp.stack([lax.axis_index("z"), lax.axis_index("g")]).astype(jnp.int32)
    adapters = planes * plane * owned
    narrow = width_local // plane

    def exchange(x, axis="g"):
        return lax.all_to_all(x, axis, split_axis=0, concat_axis=0, tiled=True)

    def mp_sum(x):
        total = x
        for k in range(1, parts):
            total = total + shift(x, "mp", parts, k)
        return total

    ids = block_adapter
    ids_all = exchange(jnp.broadcast_to(ids[None], (plane, blocks))).reshape(-1)
    up_parts = [adapter_up] + [shift(adapter_up, "z", planes, k) for k in range(1, planes)]

    down_send = adapter_down.reshape(owned, rank, plane, narrow).transpose(2, 0, 1, 3)
    down_n = exchange(down_send).reshape(plane * owned, rank, narrow)
    table = lax.all_gather(down_n, "z", axis=0, tiled=True)

    slots = exchange(select_up(ids_all, me, up_parts, owned, planes, plane))
    rg_part = rank_grad_part(ids, slots, cotangent, owned)
    rg = (adapter_scale * mp_sum(rg_part)).astype(bf)
    rg_all = [rg] + [shift(rg, "g", plane, k) for k in range(1, plane)]

    tok_send = tokens.reshape(tokens_local, plane, narrow).transpose(1, 0, 2)
    tok_n = exchange(tok_send)

    grad_table = down_terms(ids_all, me, rg_all, tok_n, adapters, rank)
    grad_n = lax.psum_scatter(grad_table, "z", scatter_dimension=0, tiled=True)
    grad_got = exchange(grad_n.reshape(plane, owned, rank, narrow))
    down_grad = grad_got.transpose(1, 2, 0, 3).reshape(owned, rank, width_local).astype(f32)

    rank_parts = exchange(rank_part(ids_all, table, tok_n))
    ranks = mp_sum(jnp.sum(rank_parts, axis=0)).astype(bf)

    through = exchange(through_down(ids_all, me, table, rg_all))
    cot_all = exchange(jnp.broadcast_to(cotangent[None], (parts,) + cotangent.shape), "mp")
    input_grad = input_gradient(cot_all, base_weight, through)

    base_part = jnp.dot(tokens, base_weight, preferred_element_type=f32)

    def columns(k):
        start = (my_mp + k) % parts * local_columns
        return lax.dynamic_slice_in_dim(base_part, start, local_columns, axis=1)

    frozen = columns(0)
    for k in range(1, parts):
        frozen = frozen + shift(columns(k).astype(bf), "mp", parts, k).astype(f32)

    output, up_send = output_and_up(ids, ranks, slots, cotangent, frozen, owned)
    up_chunks = gather_up(ids_all, me, exchange(up_send), owned)
    up_grad = up_chunks[0]
    for k in range(1, planes):
        up_grad = up_grad + shift(up_chunks[k], "z", planes, k).astype(f32)
    return (output, input_grad, down_grad, up_grad)


def solution(mesh):
    fine = Mesh(mesh.devices.reshape(-1, PLANE, mesh.devices.shape[1]), ("z", "g", "mp"))
    dp = ("z", "g")
    return jax.shard_map(
        shards,
        mesh=fine,
        in_specs=(
            P(dp, "mp"),
            P("mp", None),
            P(dp, None, "mp"),
            P(dp, None, "mp"),
            P(dp),
            P(dp, "mp"),
        ),
        out_specs=(P(dp, "mp"), P(dp, "mp"), P(dp, None, "mp"), P(dp, None, "mp")),
        check_vma=False,
    )
```

```python
import functools

import jax
import jax.numpy as jnp
from jax import lax
from jax.experimental import pallas as pl
from jax.experimental.pallas import tpu as pltpu
from jax.sharding import Mesh, PartitionSpec as P

adapter_scale = 2.0
PLANE = 8
QUAD = 4
f32, bf = jnp.float32, jnp.bfloat16

SMEM = functools.partial(pl.BlockSpec, memory_space=pltpu.SMEM)
VMEM = functools.partial(pl.BlockSpec, memory_space=pltpu.VMEM)


def diagonal(length, rank):
    rows = lax.broadcasted_iota(jnp.int32, (QUAD * length, QUAD * rank), 0) // length
    cols = lax.broadcasted_iota(jnp.int32, (QUAD * length, QUAD * rank), 1) // rank
    return rows == cols


def fold(product, mask, length):
    kept = jnp.where(mask, product, 0.0)
    total = kept[:length]
    for i in range(1, QUAD):
        total = total + kept[i * length : (i + 1) * length]
    return total


def spread(quad, mask):
    wide = jnp.concatenate([quad] * QUAD, axis=0)
    return jnp.where(mask, wide, jnp.zeros_like(wide))


def dot_nt(a, b):
    return lax.dot_general(a, b, (((1,), (1,)), ((), ())), preferred_element_type=f32)


def dot_nn(a, b):
    return lax.dot_general(a, b, (((1,), (0,)), ((), ())), preferred_element_type=f32)


def dot_tn(a, b):
    return lax.dot_general(a, b, (((0,), (0,)), ((), ())), preferred_element_type=f32)


HBM = functools.partial(pl.BlockSpec, memory_space=pl.ANY)


def stacked(count, like):
    return [pltpu.VMEM((count,) + like.shape, like.dtype), pltpu.SemaphoreType.DMA((count,))]


def load(refs, stack, sems):
    for k, ref in enumerate(refs):
        pltpu.make_async_copy(ref, stack.at[k], sems.at[k]).start()


def loaded(refs, stack, sems, k):
    pltpu.make_async_copy(refs[0], stack.at[k], sems.at[k]).wait()


def back(me, k, size):
    return lax.rem(me - k + size, size)


def select_up(ids_all, me, gathered, plane):
    planes, owned, rank, cols = gathered.shape
    blocks = ids_all.shape[0] // plane

    def kernel(ids_ref, me_ref, all_ref, out_ref):
        my_g = me_ref[1]

        def step(b, carry):
            number = ids_ref[b]
            owner = lax.div(number, owned)

            @pl.when(lax.rem(owner, plane) == my_g)
            def _():
                z = lax.div(owner, plane)
                out_ref[lax.div(b, blocks), z] = all_ref[z, lax.rem(number, owned)]

            return carry

        lax.fori_loop(0, plane * blocks, step, 0, unroll=4)

    return pl.pallas_call(
        kernel,
        in_specs=[SMEM(), SMEM(), VMEM()],
        out_specs=VMEM(),
        out_shape=jax.ShapeDtypeStruct((plane, planes, rank, cols), bf),
        name="select_up",
    )(ids_all, me, gathered)


def up_rows(ids_ref, slots_ref, q, owned, plane):
    rows = []
    for i in range(QUAD):
        owner = ids_ref[q * QUAD + i] // owned
        rows.append(slots_ref[owner % plane, owner // plane])
    return jnp.concatenate(rows, axis=0)


def rank_grad_part(ids, slots, cot, owned):
    plane, _, rank, _ = slots.shape
    blocks = ids.shape[0]
    length = cot.shape[0] // blocks
    quads = blocks // QUAD
    span = QUAD * length

    def kernel(ids_ref, slots_ref, cot_ref, out_ref):
        mask = diagonal(length, rank)
        for q in range(quads):
            up = up_rows(ids_ref, slots_ref, q, owned, plane)
            out_ref[q] = fold(dot_nt(cot_ref[q * span : (q + 1) * span, :], up), mask, length)

    return pl.pallas_call(
        kernel,
        in_specs=[SMEM(), VMEM(), VMEM()],
        out_specs=VMEM(),
        out_shape=jax.ShapeDtypeStruct((quads, length, QUAD * rank), f32),
        name="rank_grad_part",
    )(ids, slots, cot)


def down_terms(ids_all, me, rg, tok, adapters, rank):
    plane = len(rg)
    quads, length = rg[0].shape[:2]
    span = QUAD * length
    blocks = quads * QUAD
    narrow = tok[0].shape[1]

    def kernel(ids_ref, me_ref, *refs):
        rgs, toks = refs[:plane], refs[plane : 2 * plane]
        out_ref, acc, rg_stack, rg_sems, tok_stack, tok_sems = refs[2 * plane :]
        mask = diagonal(length, rank)
        load(rgs, rg_stack, rg_sems)
        load(toks, tok_stack, tok_sems)

        def clear(c, carry):
            acc[pl.ds(c * 8, 8)] = jnp.zeros((8, rank, narrow), f32)
            return carry

        lax.fori_loop(0, adapters // 8, clear, 0)

        def step(k, carry):
            loaded(rgs, rg_stack, rg_sems, k)
            loaded(toks, tok_stack, tok_sems, k)
            src = back(me_ref[1], k, plane)
            for q in range(quads):
                wide = spread(rg_stack[k, q], mask)
                rows = tok_stack[k, q * span : (q + 1) * span, :]
                got = dot_tn(wide, rows) * (1.0 / length)
                for i in range(QUAD):
                    a = ids_ref[src * blocks + q * QUAD + i]
                    acc[a] = acc[a] + got[i * rank : (i + 1) * rank]
            return carry

        lax.fori_loop(0, plane, step, 0)

        def finish(c, carry):
            out_ref[pl.ds(c * 8, 8)] = acc[pl.ds(c * 8, 8)].astype(bf)
            return carry

        lax.fori_loop(0, adapters // 8, finish, 0)

    return pl.pallas_call(
        kernel,
        in_specs=[SMEM(), SMEM()] + [HBM()] * (2 * plane),
        out_specs=VMEM(),
        out_shape=jax.ShapeDtypeStruct((adapters, rank, narrow), bf),
        scratch_shapes=[pltpu.VMEM((adapters, rank, narrow), f32)]
        + stacked(plane, rg[0])
        + stacked(plane, tok[0]),
        name="down_terms",
    )(ids_all, me, *rg, *tok)


def table_rows(ids_ref, table_ref, first):
    return jnp.concatenate([table_ref[ids_ref[first + i]] for i in range(QUAD)], axis=0)


def rank_part(ids_all, me, table, tok):
    plane = len(tok)
    tokens, _ = tok[0].shape
    rank = table.shape[1]
    blocks = ids_all.shape[0] // plane
    length = tokens // blocks
    quads = blocks // QUAD
    span = QUAD * length

    def kernel(ids_ref, me_ref, table_ref, *refs):
        toks, (out_ref, stack, sems) = refs[:plane], refs[plane:]
        mask = diagonal(length, rank)
        load(toks, stack, sems)

        def step(k, carry):
            dest = back(me_ref[1], k, plane)
            loaded(toks, stack, sems, k)
            for q in range(quads):
                down = table_rows(ids_ref, table_ref, dest * blocks + q * QUAD)
                got = dot_nt(stack[k, q * span : (q + 1) * span, :], down)
                out_ref[dest, q] = fold(got, mask, length)
            return carry

        lax.fori_loop(0, plane, step, 0)

    return pl.pallas_call(
        kernel,
        in_specs=[SMEM(), SMEM(), VMEM()] + [HBM()] * plane,
        out_specs=VMEM(),
        out_shape=jax.ShapeDtypeStruct((plane, quads, length, QUAD * rank), f32),
        scratch_shapes=stacked(plane, tok[0]),
        name="rank_part",
    )(ids_all, me, table, *tok)


def through_down(ids_all, me, table, rg):
    plane = len(rg)
    quads, length = rg[0].shape[:2]
    rank, narrow = table.shape[1:]
    span = QUAD * length
    blocks = quads * QUAD
    piece = jax.ShapeDtypeStruct((quads * span, narrow), bf)

    def kernel(ids_ref, me_ref, table_ref, *refs):
        rgs, outs = refs[:plane], refs[plane : 2 * plane]
        rg_stack, rg_sems, stack, sems = refs[2 * plane :]
        mask = diagonal(length, rank)
        load(rgs, rg_stack, rg_sems)

        def step(k, carry):
            loaded(rgs, rg_stack, rg_sems, k)
            src = back(me_ref[1], k, plane)
            for q in range(quads):
                down = table_rows(ids_ref, table_ref, src * blocks + q * QUAD)
                got = dot_nn(spread(rg_stack[k, q], mask), down)
                stack[k, q * span : (q + 1) * span, :] = got.astype(bf)
            return carry

        lax.fori_loop(0, plane, step, 0)
        for k in range(plane):
            pltpu.make_async_copy(stack.at[k], outs[k], sems.at[k]).start()
        for k in range(plane):
            pltpu.make_async_copy(stack.at[k], outs[k], sems.at[k]).wait()

    return pl.pallas_call(
        kernel,
        in_specs=[SMEM(), SMEM(), VMEM()] + [HBM()] * plane,
        out_specs=tuple([HBM()] * plane),
        out_shape=tuple([piece] * plane),
        scratch_shapes=stacked(plane, rg[0]) + stacked(plane, piece),
        name="through_down",
    )(ids_all, me, table, *rg)


def output_and_up(ids, ranks, slots, cot, base, owned):
    plane, _, rank, _ = slots.shape
    quads, length = ranks.shape[:2]
    span = QUAD * length

    def kernel(ids_ref, rank_ref, slots_ref, cot_ref, base_ref, out_ref, send_ref):
        mask = diagonal(length, rank)
        for q in range(quads):
            wide = spread(rank_ref[q], mask)
            up = up_rows(ids_ref, slots_ref, q, owned, plane)
            rows = slice(q * span, (q + 1) * span)
            out_ref[rows, :] = (base_ref[rows, :] + adapter_scale * dot_nn(wide, up)).astype(bf)
            got = (dot_tn(wide, cot_ref[rows, :]) * (adapter_scale / length)).astype(bf)
            for i in range(QUAD):
                owner = ids_ref[q * QUAD + i] // owned
                send_ref[owner % plane, owner // plane] = got[i * rank : (i + 1) * rank]

    return pl.pallas_call(
        kernel,
        in_specs=[SMEM()] + [VMEM()] * 4,
        out_specs=(VMEM(), VMEM()),
        out_shape=(
            jax.ShapeDtypeStruct(cot.shape, bf),
            jax.ShapeDtypeStruct(slots.shape, bf),
        ),
        name="output_and_up",
    )(ids, ranks, slots, cot, base)


def gather_up(ids_all, me, got, owned):
    plane, planes, rank, cols = got.shape
    blocks = ids_all.shape[0] // plane

    def kernel(ids_ref, me_ref, got_ref, *refs):
        outs, acc = refs[:planes], refs[planes]
        my_z, my_g = me_ref[0], me_ref[1]
        acc[...] = jnp.zeros(acc.shape, f32)

        def step(b, carry):
            number = ids_ref[b]
            owner = lax.div(number, owned)

            @pl.when(lax.rem(owner, plane) == my_g)
            def _():
                z, local = lax.div(owner, plane), lax.rem(number, owned)
                acc[z, local] = acc[z, local] + got_ref[lax.div(b, blocks), z].astype(f32)

            return carry

        lax.fori_loop(0, plane * blocks, step, 0, unroll=4)
        for k in range(planes):
            outs[k][...] = acc[lax.rem(my_z + k, planes)].astype(outs[k].dtype)

    chunk = (owned, rank, cols)
    return pl.pallas_call(
        kernel,
        in_specs=[SMEM(), SMEM(), VMEM()],
        out_specs=tuple([VMEM()] * planes),
        out_shape=tuple(jax.ShapeDtypeStruct(chunk, bf if k else f32) for k in range(planes)),
        scratch_shapes=[pltpu.VMEM((planes,) + chunk, f32)],
        name="gather_up",
    )(ids_all, me, got)


def base_gradient(me, cots, weight):
    parts = len(cots)
    tokens, cols = cots[0].shape
    features = weight.shape[0]
    tile = 256

    def kernel(me_ref, *refs):
        w_ref, out_ref = refs[parts], refs[parts + 1]
        total = jnp.zeros((tokens, tile), f32)
        for k in range(parts):
            first = pl.multiple_of(back(me_ref[2], k, parts) * cols, cols)
            total = total + dot_nt(refs[k][...], w_ref[:, pl.ds(first, cols)])
        out_ref[...] = total

    return pl.pallas_call(
        kernel,
        grid=(features // tile,),
        in_specs=[SMEM()]
        + [pl.BlockSpec((tokens, cols), lambda s: (0, 0))] * parts
        + [pl.BlockSpec((tile, parts * cols), lambda s: (s, 0))],
        out_specs=pl.BlockSpec((tokens, tile), lambda s: (0, s)),
        out_shape=jax.ShapeDtypeStruct((tokens, features), f32),
        name="base_gradient",
    )(me, *cots, weight)


def input_gradient(me, base, through):
    plane = len(through)
    tokens, narrow = through[0].shape

    def kernel(me_ref, base_ref, *refs):
        out_ref = refs[plane]
        for k in range(plane):
            first = pl.multiple_of(lax.rem(me_ref[1] + k, plane) * narrow, narrow)
            cols = pl.ds(first, narrow)
            out_ref[:, cols] = (base_ref[:, cols] + refs[k][...].astype(f32)).astype(bf)

    return pl.pallas_call(
        kernel,
        in_specs=[SMEM()] + [VMEM()] * (plane + 1),
        out_specs=VMEM(),
        out_shape=jax.ShapeDtypeStruct((tokens, plane * narrow), bf),
        name="input_gradient",
    )(me, base, *through)


def shift(x, axis, size, k):
    return lax.ppermute(x, axis, [(i, (i + k) % size) for i in range(size)])


def step(tokens, base_weight, adapter_down, adapter_up, block_adapter, cotangent):
    blocks = block_adapter.shape[0]
    owned, rank, width_local = adapter_down.shape
    _, local_columns = cotangent.shape
    planes, plane, parts = lax.axis_size("z"), lax.axis_size("g"), lax.axis_size("mp")
    my_mp = lax.axis_index("mp")
    my_g = lax.axis_index("g")
    me = jnp.stack([lax.axis_index("z"), my_g, my_mp]).astype(jnp.int32)
    adapters = planes * plane * owned
    narrow = width_local // plane

    def exchange(x, axis="g"):
        return lax.all_to_all(x, axis, split_axis=0, concat_axis=0, tiled=True)

    def sliced(x):
        return x.reshape(owned, rank, plane, narrow).transpose(2, 0, 1, 3)

    def mp_sum(x):
        total = x
        for k in range(1, parts):
            total = total + shift(x, "mp", parts, k)
        return total

    ids = block_adapter
    up_all = lax.all_gather(adapter_up, "z", axis=0)
    tile = jnp.pad(ids.astype(bf)[None, None], ((0, 0), (0, 15), (0, narrow - blocks)))
    sent = jnp.concatenate(
        [sliced(adapter_down).reshape(plane, owned * rank, narrow)]
        + [jnp.broadcast_to(tile, (plane, 16, narrow))],
        axis=1,
    )
    got = exchange(sent)
    ids_all = got[:, owned * rank, :blocks].astype(jnp.int32).reshape(-1)
    down_n = got[:, : owned * rank].reshape(plane * owned, rank, narrow)
    table = lax.all_gather(down_n, "z", axis=0, tiled=True)
    tok_n = []
    for k in range(plane):
        first = lax.rem(my_g + k, plane) * narrow
        part = lax.dynamic_slice_in_dim(tokens, first, narrow, axis=1)
        tok_n.append(shift(part, "g", plane, k) if k else part)
    cots = [cotangent] + [shift(cotangent, "mp", parts, k) for k in range(1, parts)]
    base_grad = base_gradient(me, cots, base_weight)
    base_part = jnp.dot(tokens, base_weight, preferred_element_type=f32)

    def columns(k):
        start = lax.rem(my_mp + k, parts) * local_columns
        return lax.dynamic_slice_in_dim(base_part, start, local_columns, axis=1)

    frozen = columns(0)
    for k in range(1, parts):
        frozen = frozen + shift(columns(k).astype(bf), "mp", parts, k).astype(f32)

    selected = select_up(ids_all, me, up_all, plane)
    slots = exchange(selected)
    rg_part = rank_grad_part(ids, slots, cotangent, owned)
    rg = (adapter_scale * mp_sum(rg_part)).astype(bf)
    rg_all = [rg] + [shift(rg, "g", plane, k) for k in range(1, plane)]

    part = rank_part(ids_all, me, table, tok_n)
    rank_parts = exchange(part)
    grad_table = down_terms(ids_all, me, rg_all, tok_n, adapters, rank)
    grad_n = lax.psum_scatter(grad_table, "z", scatter_dimension=0, tiled=True)
    grad_got = exchange(grad_n.reshape(plane, owned, rank, narrow))
    down_grad = jnp.concatenate([grad_got[i] for i in range(plane)], axis=-1).astype(f32)

    ranks = mp_sum(jnp.sum(rank_parts, axis=0)).astype(bf)

    through_n = through_down(ids_all, me, table, rg_all)
    through = [through_n[0]]
    through += [shift(through_n[k], "g", plane, plane - k) for k in range(1, plane)]
    input_grad = input_gradient(me, base_grad, through)

    output, up_send = output_and_up(ids, ranks, slots, cotangent, frozen, owned)
    up_got = exchange(up_send)
    up_chunks = gather_up(ids_all, me, up_got, owned)
    up_grad = up_chunks[0]
    for k in range(1, planes):
        up_grad = up_grad + shift(up_chunks[k], "z", planes, k).astype(f32)
    return (output, input_grad, down_grad, up_grad)


def solution(mesh):
    fine = Mesh(mesh.devices.reshape(-1, PLANE, mesh.devices.shape[1]), ("z", "g", "mp"))
    dp = ("z", "g")
    return jax.shard_map(
        step,
        mesh=fine,
        in_specs=(
            P(dp, "mp"),
            P("mp", None),
            P(dp, None, "mp"),
            P(dp, None, "mp"),
            P(dp),
            P(dp, "mp"),
        ),
        out_specs=(P(dp, "mp"), P(dp, "mp"), P(dp, None, "mp"), P(dp, None, "mp")),
        check_vma=False,
    )
```

```python
import functools

import jax
import jax.numpy as jnp
from jax import lax
from jax.experimental import pallas as pl
from jax.experimental.pallas import tpu as pltpu
from jax.sharding import Mesh, PartitionSpec as P

adapter_scale = 2.0
PLANE = 8
QUAD = 4
f32, bf = jnp.float32, jnp.bfloat16

SMEM = functools.partial(pl.BlockSpec, memory_space=pltpu.SMEM)
VMEM = functools.partial(pl.BlockSpec, memory_space=pltpu.VMEM)


def diagonal(length, rank):
    rows = lax.broadcasted_iota(jnp.int32, (QUAD * length, QUAD * rank), 0) // length
    cols = lax.broadcasted_iota(jnp.int32, (QUAD * length, QUAD * rank), 1) // rank
    return rows == cols


def fold(product, mask, length):
    kept = jnp.where(mask, product, 0.0)
    total = kept[:length]
    for i in range(1, QUAD):
        total = total + kept[i * length : (i + 1) * length]
    return total


def spread(quad, mask):
    wide = jnp.concatenate([quad] * QUAD, axis=0)
    return jnp.where(mask, wide, jnp.zeros_like(wide))


def dot_nt(a, b):
    return lax.dot_general(a, b, (((1,), (1,)), ((), ())), preferred_element_type=f32)


def dot_nn(a, b):
    return lax.dot_general(a, b, (((1,), (0,)), ((), ())), preferred_element_type=f32)


def dot_tn(a, b):
    return lax.dot_general(a, b, (((0,), (0,)), ((), ())), preferred_element_type=f32)


HBM = functools.partial(pl.BlockSpec, memory_space=pl.ANY)


def stacked(count, like):
    return [pltpu.VMEM((count,) + like.shape, like.dtype), pltpu.SemaphoreType.DMA((count,))]


def load(refs, stack, sems):
    for k, ref in enumerate(refs):
        pltpu.make_async_copy(ref, stack.at[k], sems.at[k]).start()


def loaded(refs, stack, sems, k):
    pltpu.make_async_copy(refs[0], stack.at[k], sems.at[k]).wait()


def back(me, k, size):
    return lax.rem(me - k + size, size)


def select_up(ids_all, me, gathered, plane):
    planes, owned, rank, cols = gathered.shape
    blocks = ids_all.shape[0] // plane

    def kernel(ids_ref, me_ref, all_ref, out_ref):
        my_g = me_ref[1]

        def step(b, carry):
            number = ids_ref[b]
            owner = lax.div(number, owned)

            @pl.when(lax.rem(owner, plane) == my_g)
            def _():
                z = lax.div(owner, plane)
                dest = back(my_g, lax.div(b, blocks), plane)
                out_ref[dest, z] = all_ref[z, lax.rem(number, owned)]

            return carry

        lax.fori_loop(0, plane * blocks, step, 0, unroll=2)

    return pl.pallas_call(
        kernel,
        in_specs=[SMEM(), SMEM(), VMEM()],
        out_specs=VMEM(),
        out_shape=jax.ShapeDtypeStruct((plane, planes, rank, cols), bf),
        name="select_up",
    )(ids_all, me, gathered)


def up_rows(ids_ref, slots_ref, q, owned, plane):
    rows = []
    for i in range(QUAD):
        owner = ids_ref[q * QUAD + i] // owned
        rows.append(slots_ref[owner % plane, owner // plane])
    return jnp.concatenate(rows, axis=0)


def rank_grad_part(ids, slots, cot, owned):
    plane, _, rank, _ = slots.shape
    blocks = ids.shape[0]
    length = cot.shape[0] // blocks
    quads = blocks // QUAD
    span = QUAD * length

    def kernel(ids_ref, slots_ref, cot_ref, out_ref):
        mask = diagonal(length, rank)
        for q in range(quads):
            up = up_rows(ids_ref, slots_ref, q, owned, plane)
            out_ref[q] = fold(dot_nt(cot_ref[q * span : (q + 1) * span, :], up), mask, length)

    return pl.pallas_call(
        kernel,
        in_specs=[SMEM(), VMEM(), VMEM()],
        out_specs=VMEM(),
        out_shape=jax.ShapeDtypeStruct((quads, length, QUAD * rank), f32),
        name="rank_grad_part",
    )(ids, slots, cot)


def down_terms(ids_all, me, rg, tok, adapters, rank):
    plane = len(rg)
    quads, length = rg[0].shape[:2]
    span = QUAD * length
    blocks = quads * QUAD
    narrow = tok[0].shape[1]

    def kernel(ids_ref, me_ref, *refs):
        rgs, toks = refs[:plane], refs[plane : 2 * plane]
        out_ref, acc, rg_stack, rg_sems, tok_stack, tok_sems = refs[2 * plane :]
        mask = diagonal(length, rank)
        load(rgs, rg_stack, rg_sems)
        load(toks, tok_stack, tok_sems)

        def clear(c, carry):
            acc[pl.ds(c * 8, 8)] = jnp.zeros((8, rank, narrow), f32)
            return carry

        lax.fori_loop(0, adapters // 8, clear, 0)

        def step(k, carry):
            loaded(rgs, rg_stack, rg_sems, k)
            loaded(toks, tok_stack, tok_sems, k)
            for q in range(quads):
                wide = spread(rg_stack[k, q], mask)
                rows = tok_stack[k, q * span : (q + 1) * span, :]
                got = dot_tn(wide, rows) * (1.0 / length)
                for i in range(QUAD):
                    a = ids_ref[k * blocks + q * QUAD + i]
                    acc[a] = acc[a] + got[i * rank : (i + 1) * rank]
            return carry

        lax.fori_loop(0, plane, step, 0)

        def finish(c, carry):
            out_ref[pl.ds(c * 8, 8)] = acc[pl.ds(c * 8, 8)].astype(bf)
            return carry

        lax.fori_loop(0, adapters // 8, finish, 0)

    return pl.pallas_call(
        kernel,
        in_specs=[SMEM(), SMEM()] + [HBM()] * (2 * plane),
        out_specs=VMEM(),
        out_shape=jax.ShapeDtypeStruct((adapters, rank, narrow), bf),
        scratch_shapes=[pltpu.VMEM((adapters, rank, narrow), f32)]
        + stacked(plane, rg[0])
        + stacked(plane, tok[0]),
        name="down_terms",
    )(ids_all, me, *rg, *tok)


def table_rows(ids_ref, table_ref, first):
    return jnp.concatenate([table_ref[ids_ref[first + i]] for i in range(QUAD)], axis=0)


def rank_part(ids_all, me, table, tok):
    plane = len(tok)
    tokens, _ = tok[0].shape
    rank = table.shape[1]
    blocks = ids_all.shape[0] // plane
    length = tokens // blocks
    quads = blocks // QUAD
    span = QUAD * length

    def kernel(ids_ref, me_ref, table_ref, *refs):
        toks, (out_ref, stack, sems) = refs[:plane], refs[plane:]
        mask = diagonal(length, rank)
        load(toks, stack, sems)

        def step(k, carry):
            dest = back(me_ref[1], k, plane)
            loaded(toks, stack, sems, k)
            for q in range(quads):
                down = table_rows(ids_ref, table_ref, k * blocks + q * QUAD)
                got = dot_nt(stack[k, q * span : (q + 1) * span, :], down)
                out_ref[dest, q] = fold(got, mask, length)
            return carry

        lax.fori_loop(0, plane, step, 0)

    return pl.pallas_call(
        kernel,
        in_specs=[SMEM(), SMEM(), VMEM()] + [HBM()] * plane,
        out_specs=VMEM(),
        out_shape=jax.ShapeDtypeStruct((plane, quads, length, QUAD * rank), f32),
        scratch_shapes=stacked(plane, tok[0]),
        name="rank_part",
    )(ids_all, me, table, *tok)


def through_down(ids_all, me, table, rg):
    plane = len(rg)
    quads, length = rg[0].shape[:2]
    rank, narrow = table.shape[1:]
    span = QUAD * length
    blocks = quads * QUAD
    piece = jax.ShapeDtypeStruct((quads * span, narrow), bf)

    def kernel(ids_ref, me_ref, table_ref, *refs):
        rgs, outs = refs[:plane], refs[plane : 2 * plane]
        rg_stack, rg_sems, stack, sems = refs[2 * plane :]
        mask = diagonal(length, rank)
        load(rgs, rg_stack, rg_sems)

        def step(k, carry):
            loaded(rgs, rg_stack, rg_sems, k)
            for q in range(quads):
                down = table_rows(ids_ref, table_ref, k * blocks + q * QUAD)
                got = dot_nn(spread(rg_stack[k, q], mask), down)
                stack[k, q * span : (q + 1) * span, :] = got.astype(bf)
            return carry

        lax.fori_loop(0, plane, step, 0)
        for k in range(plane):
            pltpu.make_async_copy(stack.at[k], outs[k], sems.at[k]).start()
        for k in range(plane):
            pltpu.make_async_copy(stack.at[k], outs[k], sems.at[k]).wait()

    return pl.pallas_call(
        kernel,
        in_specs=[SMEM(), SMEM(), VMEM()] + [HBM()] * plane,
        out_specs=tuple([HBM()] * plane),
        out_shape=tuple([piece] * plane),
        scratch_shapes=stacked(plane, rg[0]) + stacked(plane, piece),
        name="through_down",
    )(ids_all, me, table, *rg)


def output_and_up(ids, ranks, slots, cot, base, owned):
    plane, _, rank, _ = slots.shape
    quads, length = ranks.shape[:2]
    span = QUAD * length

    def kernel(ids_ref, rank_ref, slots_ref, cot_ref, base_ref, out_ref, send_ref):
        mask = diagonal(length, rank)
        for q in range(quads):
            wide = spread(rank_ref[q], mask)
            up = up_rows(ids_ref, slots_ref, q, owned, plane)
            rows = slice(q * span, (q + 1) * span)
            out_ref[rows, :] = (base_ref[rows, :] + adapter_scale * dot_nn(wide, up)).astype(bf)
            got = (dot_tn(wide, cot_ref[rows, :]) * (adapter_scale / length)).astype(bf)
            for i in range(QUAD):
                owner = ids_ref[q * QUAD + i] // owned
                send_ref[owner % plane, owner // plane] = got[i * rank : (i + 1) * rank]

    return pl.pallas_call(
        kernel,
        in_specs=[SMEM()] + [VMEM()] * 4,
        out_specs=(VMEM(), VMEM()),
        out_shape=(
            jax.ShapeDtypeStruct(cot.shape, bf),
            jax.ShapeDtypeStruct(slots.shape, bf),
        ),
        name="output_and_up",
    )(ids, ranks, slots, cot, base)


def gather_up(ids_all, me, got, owned):
    plane, planes, rank, cols = got.shape
    blocks = ids_all.shape[0] // plane

    def kernel(ids_ref, me_ref, got_ref, out_ref, acc):
        my_g = me_ref[1]
        acc[...] = jnp.zeros(acc.shape, f32)

        def step(b, carry):
            number = ids_ref[b]
            owner = lax.div(number, owned)

            @pl.when(lax.rem(owner, plane) == my_g)
            def _():
                z, local = lax.div(owner, plane), lax.rem(number, owned)
                acc[z, local] = acc[z, local] + got_ref[back(my_g, lax.div(b, blocks), plane), z].astype(f32)

            return carry

        lax.fori_loop(0, plane * blocks, step, 0, unroll=2)
        out_ref[...] = acc[...].astype(bf)

    shape = (planes, owned, rank, cols)
    return pl.pallas_call(
        kernel,
        in_specs=[SMEM(), SMEM(), VMEM()],
        out_specs=VMEM(),
        out_shape=jax.ShapeDtypeStruct(shape, bf),
        scratch_shapes=[pltpu.VMEM(shape, f32)],
        name="gather_up",
    )(ids_all, me, got)


def input_gradient(me, cots, weight, through):
    parts, plane = len(cots), len(through)
    tokens, cols = cots[0].shape
    narrow = through[0].shape[1]

    def ahead(i, me_ref):
        return lax.rem(me_ref[1] + i, plane)

    def kernel(me_ref, *refs):
        cot_refs, w_ref, thr_refs = refs[:parts], refs[parts], refs[parts + 1 : parts + 1 + plane]
        out_ref, stack, sems = refs[parts + 1 + plane :]
        i = pl.program_id(0)

        @pl.when(i == 0)
        def _():
            load(thr_refs, stack, sems)

        loaded(thr_refs, stack, sems, i)
        total = stack[i].astype(f32)
        for k in range(parts):
            first = pl.multiple_of(back(me_ref[2], k, parts) * cols, cols)
            total = total + dot_nt(cot_refs[k][...], w_ref[:, pl.ds(first, cols)])
        out_ref[...] = total.astype(bf)

    return pl.pallas_call(
        kernel,
        grid_spec=pltpu.PrefetchScalarGridSpec(
            num_scalar_prefetch=1,
            grid=(plane,),
            in_specs=[pl.BlockSpec((tokens, cols), lambda i, me_ref: (0, 0))] * parts
            + [pl.BlockSpec((narrow, parts * cols), lambda i, me_ref: (ahead(i, me_ref), 0))]
            + [HBM()] * plane,
            out_specs=pl.BlockSpec((tokens, narrow), lambda i, me_ref: (0, ahead(i, me_ref))),
            scratch_shapes=stacked(plane, through[0]),
        ),
        out_shape=jax.ShapeDtypeStruct((tokens, plane * narrow), bf),
        name="input_gradient",
    )(me, *cots, weight, *through)


def pack_down(me, down, tile, plane):
    rows, width = down.shape
    narrow = width // plane
    piece = jax.ShapeDtypeStruct((rows + tile.shape[0], narrow), bf)

    def kernel(me_ref, down_ref, tile_ref, *outs):
        for k in range(plane):
            first = pl.multiple_of(lax.rem(me_ref[1] + k, plane) * narrow, narrow)
            outs[k][:rows, :] = down_ref[:, pl.ds(first, narrow)]
            outs[k][rows:, :] = tile_ref[...]

    return pl.pallas_call(
        kernel,
        in_specs=[SMEM(), VMEM(), VMEM()],
        out_specs=tuple([VMEM()] * plane),
        out_shape=tuple([piece] * plane),
        name="pack_down",
    )(me, down, tile)


def unpack_down(pieces, rows):
    plane = len(pieces)
    narrow = pieces[0].shape[1]

    def kernel(*refs):
        down_ref, ids_ref = refs[plane:]
        for k in range(plane):
            down_ref[k] = refs[k][:rows, :]
            ids_ref[k : k + 1, :] = refs[k][rows : rows + 1, :128].astype(f32).astype(jnp.int32)

    return pl.pallas_call(
        kernel,
        in_specs=[VMEM()] * plane,
        out_specs=(VMEM(), VMEM()),
        out_shape=(
            jax.ShapeDtypeStruct((plane, rows, narrow), bf),
            jax.ShapeDtypeStruct((plane, 128), jnp.int32),
        ),
        name="unpack_down",
    )(*pieces)


def down_gradient(me, pieces):
    plane = len(pieces)
    owned, rank, narrow = pieces[0].shape

    def kernel(me_ref, *refs):
        out_ref = refs[plane]
        for k in range(plane):
            first = pl.multiple_of(back(me_ref[1], k, plane) * narrow, narrow)
            out_ref[:, :, pl.ds(first, narrow)] = refs[k][...].astype(f32)

    return pl.pallas_call(
        kernel,
        in_specs=[SMEM()] + [VMEM()] * plane,
        out_specs=VMEM(),
        out_shape=jax.ShapeDtypeStruct((owned, rank, plane * narrow), f32),
        name="down_gradient",
    )(me, *pieces)


def shift(x, axis, size, k):
    return lax.ppermute(x, axis, [(i, (i + k) % size) for i in range(size)])


def step(tokens, base_weight, adapter_down, adapter_up, block_adapter, cotangent):
    blocks = block_adapter.shape[0]
    owned, rank, width_local = adapter_down.shape
    _, local_columns = cotangent.shape
    planes, plane, parts = lax.axis_size("z"), lax.axis_size("g"), lax.axis_size("mp")
    my_mp = lax.axis_index("mp")
    my_g = lax.axis_index("g")
    me = jnp.stack([lax.axis_index("z"), my_g, my_mp]).astype(jnp.int32)
    adapters = planes * plane * owned
    narrow = width_local // plane

    def exchange(x, axis="g"):
        return lax.all_to_all(x, axis, split_axis=0, concat_axis=0, tiled=True)

    def mp_sum(x):
        total = x
        for k in range(1, parts):
            total = total + shift(x, "mp", parts, k)
        return total

    ids = block_adapter
    up_all = exchange(jnp.broadcast_to(adapter_up[None], (planes,) + adapter_up.shape), "z")
    rows = owned * rank
    tile = jnp.pad(ids.astype(bf)[None], ((0, 15), (0, narrow - blocks)))
    packed = pack_down(me, adapter_down.reshape(rows, width_local), tile, plane)
    got = [packed[0]] + [shift(packed[k], "g", plane, k) for k in range(1, plane)]
    down_n, ids_rows = unpack_down(got, rows)
    table = lax.all_gather(down_n.reshape(-1, rank, narrow), "z", axis=0, tiled=True)
    ids_all = ids_rows[:, :blocks].reshape(-1)
    owner = ids_all // owned
    steps = lax.rem(my_g - owner % plane + plane, plane)
    ids_row = (owner // plane * plane + steps) * owned + ids_all % owned
    tok_n = []
    for k in range(plane):
        first = lax.rem(my_g + k, plane) * narrow
        part = lax.dynamic_slice_in_dim(tokens, first, narrow, axis=1)
        tok_n.append(shift(part, "g", plane, k) if k else part)
    cots = [cotangent] + [shift(cotangent, "mp", parts, k) for k in range(1, parts)]
    base_part = jnp.dot(tokens, base_weight, preferred_element_type=f32)

    def columns(k):
        start = lax.rem(my_mp + k, parts) * local_columns
        return lax.dynamic_slice_in_dim(base_part, start, local_columns, axis=1)

    frozen = columns(0)
    for k in range(1, parts):
        frozen = frozen + shift(columns(k).astype(bf), "mp", parts, k).astype(f32)

    selected = select_up(ids_all, me, up_all, plane)
    slots = exchange(selected)
    rg_part = rank_grad_part(ids, slots, cotangent, owned)
    rg = (adapter_scale * mp_sum(rg_part)).astype(bf)
    rg_all = [rg] + [shift(rg, "g", plane, k) for k in range(1, plane)]

    part = rank_part(ids_row, me, table, tok_n)
    rank_parts = exchange(part)
    grad_table = down_terms(ids_all, me, rg_all, tok_n, adapters, rank)
    grad_n = lax.psum_scatter(grad_table, "z", scatter_dimension=0, tiled=True)
    chunks = grad_n.reshape(plane, owned, rank, narrow)
    grad_got = []
    for k in range(plane):
        part = lax.dynamic_index_in_dim(chunks, lax.rem(my_g + k, plane), 0, keepdims=False)
        grad_got.append(shift(part, "g", plane, k) if k else part)
    down_grad = down_gradient(me, grad_got)

    ranks = mp_sum(jnp.sum(rank_parts, axis=0)).astype(bf)

    through_n = through_down(ids_row, me, table, rg_all)
    through = [through_n[0]]
    through += [shift(through_n[k], "g", plane, plane - k) for k in range(1, plane)]
    input_grad = input_gradient(me, cots, base_weight, through)

    output, up_send = output_and_up(ids, ranks, slots, cotangent, frozen, owned)
    up_got = exchange(up_send)
    up_chunks = gather_up(ids_all, me, up_got, owned)
    up_got = exchange(up_chunks, "z")
    up_grad = jnp.sum(up_got.astype(f32), axis=0)
    return (output, input_grad, down_grad, up_grad)


def solution(mesh):
    fine = Mesh(mesh.devices.reshape(-1, PLANE, mesh.devices.shape[1]), ("z", "g", "mp"))
    dp = ("z", "g")
    return jax.shard_map(
        step,
        mesh=fine,
        in_specs=(
            P(dp, "mp"),
            P("mp", None),
            P(dp, None, "mp"),
            P(dp, None, "mp"),
            P(dp),
            P(dp, "mp"),
        ),
        out_specs=(P(dp, "mp"), P(dp, "mp"), P(dp, None, "mp"), P(dp, None, "mp")),
        check_vma=False,
    )
```

```python
import functools

import jax
import jax.numpy as jnp
from jax import lax
from jax.experimental import pallas as pl
from jax.experimental.pallas import tpu as pltpu
from jax.sharding import Mesh, PartitionSpec as P

adapter_scale = 2.0
PLANE = 8
QUAD = 4
f32, bf = jnp.float32, jnp.bfloat16

SMEM = functools.partial(pl.BlockSpec, memory_space=pltpu.SMEM)
VMEM = functools.partial(pl.BlockSpec, memory_space=pltpu.VMEM)


def diagonal(length, rank):
    rows = lax.broadcasted_iota(jnp.int32, (QUAD * length, QUAD * rank), 0) // length
    cols = lax.broadcasted_iota(jnp.int32, (QUAD * length, QUAD * rank), 1) // rank
    return rows == cols


def fold(product, mask, length):
    kept = jnp.where(mask, product, 0.0)
    total = kept[:length]
    for i in range(1, QUAD):
        total = total + kept[i * length : (i + 1) * length]
    return total


def spread(quad, mask):
    wide = jnp.concatenate([quad] * QUAD, axis=0)
    return jnp.where(mask, wide, jnp.zeros_like(wide))


def dot_nt(a, b):
    return lax.dot_general(a, b, (((1,), (1,)), ((), ())), preferred_element_type=f32)


def dot_nn(a, b):
    return lax.dot_general(a, b, (((1,), (0,)), ((), ())), preferred_element_type=f32)


def dot_tn(a, b):
    return lax.dot_general(a, b, (((0,), (0,)), ((), ())), preferred_element_type=f32)


HBM = functools.partial(pl.BlockSpec, memory_space=pl.ANY)


def stacked(count, like):
    return [pltpu.VMEM((count,) + like.shape, like.dtype), pltpu.SemaphoreType.DMA((count,))]


def load(refs, stack, sems):
    for k, ref in enumerate(refs):
        pltpu.make_async_copy(ref, stack.at[k], sems.at[k]).start()


def loaded(refs, stack, sems, k):
    pltpu.make_async_copy(refs[0], stack.at[k], sems.at[k]).wait()


def divide(x, n):
    return x >> (n.bit_length() - 1) if n & (n - 1) == 0 else lax.div(x, n)


def remainder(x, n):
    return x & (n - 1) if n & (n - 1) == 0 else lax.rem(x, n)


def back(me, k, size):
    return remainder(me - k + size, size)


def select_up(ids_all, me, gathered, plane):
    planes, owned, rank, cols = gathered.shape
    blocks = ids_all.shape[0] // plane

    def kernel(ids_ref, me_ref, all_ref, out_ref):
        my_g = me_ref[1]

        def step(b, carry):
            number = ids_ref[b]
            owner = divide(number, owned)

            @pl.when(remainder(owner, plane) == my_g)
            def _():
                z = divide(owner, plane)
                dest = back(my_g, divide(b, blocks), plane)
                out_ref[dest, z] = all_ref[z, remainder(number, owned)]

            return carry

        lax.fori_loop(0, plane * blocks, step, 0, unroll=2)

    return pl.pallas_call(
        kernel,
        in_specs=[SMEM(), SMEM(), VMEM()],
        out_specs=VMEM(),
        out_shape=jax.ShapeDtypeStruct((plane, planes, rank, cols), bf),
        name="select_up",
    )(ids_all, me, gathered)


def up_rows(ids_ref, slots_ref, q, owned, plane):
    rows = []
    for i in range(QUAD):
        owner = divide(ids_ref[q * QUAD + i], owned)
        rows.append(slots_ref[remainder(owner, plane), divide(owner, plane)])
    return jnp.concatenate(rows, axis=0)


def rank_grad_part(ids, slots, cot, owned):
    plane, _, rank, _ = slots.shape
    blocks = ids.shape[0]
    length = cot.shape[0] // blocks
    quads = blocks // QUAD
    span = QUAD * length

    def kernel(ids_ref, slots_ref, cot_ref, out_ref):
        mask = diagonal(length, rank)
        for q in range(quads):
            up = up_rows(ids_ref, slots_ref, q, owned, plane)
            out_ref[q] = fold(dot_nt(cot_ref[q * span : (q + 1) * span, :], up), mask, length)

    return pl.pallas_call(
        kernel,
        in_specs=[SMEM(), VMEM(), VMEM()],
        out_specs=VMEM(),
        out_shape=jax.ShapeDtypeStruct((quads, length, QUAD * rank), f32),
        name="rank_grad_part",
    )(ids, slots, cot)


def down_terms(ids_all, me, rg, tok, adapters, rank):
    plane = len(rg)
    quads, length = rg[0].shape[:2]
    span = QUAD * length
    blocks = quads * QUAD
    narrow = tok[0].shape[1]

    def kernel(ids_ref, me_ref, *refs):
        rgs, toks = refs[:plane], refs[plane : 2 * plane]
        out_ref, acc, rg_stack, rg_sems, tok_stack, tok_sems = refs[2 * plane :]
        mask = diagonal(length, rank)
        load(rgs, rg_stack, rg_sems)
        load(toks, tok_stack, tok_sems)

        def clear(c, carry):
            acc[pl.ds(c * 8, 8)] = jnp.zeros((8, rank, narrow), f32)
            return carry

        lax.fori_loop(0, adapters // 8, clear, 0)

        def step(k, carry):
            loaded(rgs, rg_stack, rg_sems, k)
            loaded(toks, tok_stack, tok_sems, k)
            for q in range(quads):
                wide = spread(rg_stack[k, q], mask)
                rows = tok_stack[k, q * span : (q + 1) * span, :]
                got = dot_tn(wide, rows) * (1.0 / length)
                for i in range(QUAD):
                    a = ids_ref[k * blocks + q * QUAD + i]
                    acc[a] = acc[a] + got[i * rank : (i + 1) * rank]
            return carry

        lax.fori_loop(0, plane, step, 0)

        def finish(c, carry):
            out_ref[pl.ds(c * 8, 8)] = acc[pl.ds(c * 8, 8)].astype(bf)
            return carry

        lax.fori_loop(0, adapters // 8, finish, 0)

    return pl.pallas_call(
        kernel,
        in_specs=[SMEM(), SMEM()] + [HBM()] * (2 * plane),
        out_specs=VMEM(),
        out_shape=jax.ShapeDtypeStruct((adapters, rank, narrow), bf),
        scratch_shapes=[pltpu.VMEM((adapters, rank, narrow), f32)]
        + stacked(plane, rg[0])
        + stacked(plane, tok[0]),
        name="down_terms",
    )(ids_all, me, *rg, *tok)


def table_rows(ids_ref, table_ref, first):
    return jnp.concatenate([table_ref[ids_ref[first + i]] for i in range(QUAD)], axis=0)


def rank_part(ids_all, me, table, tok):
    plane = len(tok)
    tokens, _ = tok[0].shape
    rank = table.shape[1]
    blocks = ids_all.shape[0] // plane
    length = tokens // blocks
    quads = blocks // QUAD
    span = QUAD * length

    def kernel(ids_ref, me_ref, table_ref, *refs):
        toks, (out_ref, stack, sems) = refs[:plane], refs[plane:]
        mask = diagonal(length, rank)
        load(toks, stack, sems)

        def step(k, carry):
            dest = back(me_ref[1], k, plane)
            loaded(toks, stack, sems, k)
            for q in range(quads):
                down = table_rows(ids_ref, table_ref, k * blocks + q * QUAD)
                got = dot_nt(stack[k, q * span : (q + 1) * span, :], down)
                out_ref[dest, q] = fold(got, mask, length).astype(bf)
            return carry

        lax.fori_loop(0, plane, step, 0)

    return pl.pallas_call(
        kernel,
        in_specs=[SMEM(), SMEM(), VMEM()] + [HBM()] * plane,
        out_specs=VMEM(),
        out_shape=jax.ShapeDtypeStruct((plane, quads, length, QUAD * rank), bf),
        scratch_shapes=stacked(plane, tok[0]),
        name="rank_part",
    )(ids_all, me, table, *tok)


def through_down(ids_all, me, table, rg):
    plane = len(rg)
    quads, length = rg[0].shape[:2]
    rank, narrow = table.shape[1:]
    span = QUAD * length
    blocks = quads * QUAD
    piece = jax.ShapeDtypeStruct((quads * span, narrow), bf)

    def kernel(ids_ref, me_ref, table_ref, *refs):
        rgs, outs = refs[:plane], refs[plane : 2 * plane]
        rg_stack, rg_sems, stack, sems = refs[2 * plane :]
        mask = diagonal(length, rank)
        load(rgs, rg_stack, rg_sems)

        def step(k, carry):
            loaded(rgs, rg_stack, rg_sems, k)
            for q in range(quads):
                down = table_rows(ids_ref, table_ref, k * blocks + q * QUAD)
                got = dot_nn(spread(rg_stack[k, q], mask), down)
                stack[k, q * span : (q + 1) * span, :] = got.astype(bf)
            return carry

        lax.fori_loop(0, plane, step, 0)
        for k in range(plane):
            pltpu.make_async_copy(stack.at[k], outs[k], sems.at[k]).start()
        for k in range(plane):
            pltpu.make_async_copy(stack.at[k], outs[k], sems.at[k]).wait()

    return pl.pallas_call(
        kernel,
        in_specs=[SMEM(), SMEM(), VMEM()] + [HBM()] * plane,
        out_specs=tuple([HBM()] * plane),
        out_shape=tuple([piece] * plane),
        scratch_shapes=stacked(plane, rg[0]) + stacked(plane, piece),
        name="through_down",
    )(ids_all, me, table, *rg)


def output_and_up(ids, ranks, slots, cot, base, owned):
    plane, _, rank, _ = slots.shape
    quads, length = ranks.shape[:2]
    span = QUAD * length

    def kernel(ids_ref, rank_ref, slots_ref, cot_ref, base_ref, out_ref, send_ref):
        mask = diagonal(length, rank)
        for q in range(quads):
            wide = spread(rank_ref[q], mask)
            up = up_rows(ids_ref, slots_ref, q, owned, plane)
            rows = slice(q * span, (q + 1) * span)
            out_ref[rows, :] = (base_ref[rows, :] + adapter_scale * dot_nn(wide, up)).astype(bf)
            got = (dot_tn(wide, cot_ref[rows, :]) * (adapter_scale / length)).astype(bf)
            for i in range(QUAD):
                owner = divide(ids_ref[q * QUAD + i], owned)
                send_ref[remainder(owner, plane), divide(owner, plane)] = got[i * rank : (i + 1) * rank]

    return pl.pallas_call(
        kernel,
        in_specs=[SMEM()] + [VMEM()] * 4,
        out_specs=(VMEM(), VMEM()),
        out_shape=(
            jax.ShapeDtypeStruct(cot.shape, bf),
            jax.ShapeDtypeStruct(slots.shape, bf),
        ),
        name="output_and_up",
    )(ids, ranks, slots, cot, base)


def gather_up(ids_all, me, got, owned):
    plane, planes, rank, cols = got.shape
    blocks = ids_all.shape[0] // plane

    def kernel(ids_ref, me_ref, got_ref, out_ref, acc):
        my_g = me_ref[1]
        acc[...] = jnp.zeros(acc.shape, f32)

        def step(b, carry):
            number = ids_ref[b]
            owner = divide(number, owned)

            @pl.when(remainder(owner, plane) == my_g)
            def _():
                z, local = divide(owner, plane), remainder(number, owned)
                acc[z, local] = acc[z, local] + got_ref[back(my_g, divide(b, blocks), plane), z].astype(f32)

            return carry

        lax.fori_loop(0, plane * blocks, step, 0, unroll=2)
        out_ref[...] = acc[...].astype(bf)

    shape = (planes, owned, rank, cols)
    return pl.pallas_call(
        kernel,
        in_specs=[SMEM(), SMEM(), VMEM()],
        out_specs=VMEM(),
        out_shape=jax.ShapeDtypeStruct(shape, bf),
        scratch_shapes=[pltpu.VMEM(shape, f32)],
        name="gather_up",
    )(ids_all, me, got)


def input_gradient(me, cots, weight, through):
    parts, plane = len(cots), len(through)
    tokens, cols = cots[0].shape
    narrow = through[0].shape[1]

    def ahead(i, me_ref):
        return lax.rem(me_ref[1] + i, plane)

    def kernel(me_ref, *refs):
        cot_refs, w_ref, thr_refs = refs[:parts], refs[parts], refs[parts + 1 : parts + 1 + plane]
        out_ref, stack, sems, whole = refs[parts + 1 + plane :]
        i = pl.program_id(0)

        @pl.when(i == 0)
        def _():
            load(thr_refs, stack, sems)
            for k in range(parts):
                first = pl.multiple_of(back(me_ref[2], k, parts) * cols, cols)
                whole[:, pl.ds(first, cols)] = cot_refs[k][...]

        loaded(thr_refs, stack, sems, i)
        out_ref[...] = (dot_nt(whole[...], w_ref[...]) + stack[i].astype(f32)).astype(bf)

    return pl.pallas_call(
        kernel,
        grid_spec=pltpu.PrefetchScalarGridSpec(
            num_scalar_prefetch=1,
            grid=(plane,),
            in_specs=[pl.BlockSpec((tokens, cols), lambda i, me_ref: (0, 0))] * parts
            + [pl.BlockSpec((narrow, parts * cols), lambda i, me_ref: (ahead(i, me_ref), 0))]
            + [HBM()] * plane,
            out_specs=pl.BlockSpec((tokens, narrow), lambda i, me_ref: (0, ahead(i, me_ref))),
            scratch_shapes=stacked(plane, through[0])
            + [pltpu.VMEM((tokens, parts * cols), bf)],
        ),
        out_shape=jax.ShapeDtypeStruct((tokens, plane * narrow), bf),
        name="input_gradient",
    )(me, *cots, weight, *through)


def pack_down(me, down, tile, plane):
    rows, width = down.shape
    narrow = width // plane
    piece = jax.ShapeDtypeStruct((rows + tile.shape[0], narrow), bf)

    def kernel(me_ref, down_ref, tile_ref, *outs):
        for k in range(plane):
            first = pl.multiple_of(lax.rem(me_ref[1] + k, plane) * narrow, narrow)
            outs[k][:rows, :] = down_ref[:, pl.ds(first, narrow)]
            outs[k][rows:, :] = tile_ref[...]

    return pl.pallas_call(
        kernel,
        in_specs=[SMEM(), VMEM(), VMEM()],
        out_specs=tuple([VMEM()] * plane),
        out_shape=tuple([piece] * plane),
        name="pack_down",
    )(me, down, tile)


def unpack_down(pieces, rows):
    plane = len(pieces)
    narrow = pieces[0].shape[1]

    def kernel(*refs):
        down_ref, ids_ref = refs[plane:]
        for k in range(plane):
            down_ref[k] = refs[k][:rows, :]
            ids_ref[k : k + 1, :] = refs[k][rows : rows + 1, :128].astype(f32).astype(jnp.int32)

    return pl.pallas_call(
        kernel,
        in_specs=[VMEM()] * plane,
        out_specs=(VMEM(), VMEM()),
        out_shape=(
            jax.ShapeDtypeStruct((plane, rows, narrow), bf),
            jax.ShapeDtypeStruct((plane, 128), jnp.int32),
        ),
        name="unpack_down",
    )(*pieces)


def down_gradient(me, pieces):
    plane = len(pieces)
    owned, rank, narrow = pieces[0].shape

    def kernel(me_ref, *refs):
        out_ref = refs[plane]
        for k in range(plane):
            first = pl.multiple_of(back(me_ref[1], k, plane) * narrow, narrow)
            out_ref[:, :, pl.ds(first, narrow)] = refs[k][...].astype(f32)

    return pl.pallas_call(
        kernel,
        in_specs=[SMEM()] + [VMEM()] * plane,
        out_specs=VMEM(),
        out_shape=jax.ShapeDtypeStruct((owned, rank, plane * narrow), f32),
        name="down_gradient",
    )(me, *pieces)


def shift(x, axis, size, k):
    return lax.ppermute(x, axis, [(i, (i + k) % size) for i in range(size)])


def step(tokens, base_weight, adapter_down, adapter_up, block_adapter, cotangent):
    blocks = block_adapter.shape[0]
    owned, rank, width_local = adapter_down.shape
    _, local_columns = cotangent.shape
    planes, plane, parts = lax.axis_size("z"), lax.axis_size("g"), lax.axis_size("mp")
    my_mp = lax.axis_index("mp")
    my_g = lax.axis_index("g")
    me = jnp.stack([lax.axis_index("z"), my_g, my_mp]).astype(jnp.int32)
    adapters = planes * plane * owned
    narrow = width_local // plane

    def exchange(x, axis="g"):
        return lax.all_to_all(x, axis, split_axis=0, concat_axis=0, tiled=True)

    def mp_sum(x):
        total = x
        for k in range(1, parts):
            total = total + shift(x, "mp", parts, k)
        return total

    ids = block_adapter
    up_all = exchange(jnp.broadcast_to(adapter_up[None], (planes,) + adapter_up.shape), "z")
    rows = owned * rank
    tile = jnp.pad(ids.astype(bf)[None], ((0, 15), (0, narrow - blocks)))
    packed = pack_down(me, adapter_down.reshape(rows, width_local), tile, plane)
    got = [packed[0]] + [shift(packed[k], "g", plane, k) for k in range(1, plane)]
    down_n, ids_rows = unpack_down(got, rows)
    table = lax.all_gather(down_n.reshape(-1, rank, narrow), "z", axis=0, tiled=True)
    ids_all = ids_rows[:, :blocks].reshape(-1)
    owner = ids_all // owned
    steps = lax.rem(my_g - owner % plane + plane, plane)
    ids_row = (owner // plane * plane + steps) * owned + ids_all % owned
    tok_n = []
    for k in range(plane):
        first = lax.rem(my_g + k, plane) * narrow
        part = lax.dynamic_slice_in_dim(tokens, first, narrow, axis=1)
        tok_n.append(shift(part, "g", plane, k) if k else part)
    cots = [cotangent] + [shift(cotangent, "mp", parts, k) for k in range(1, parts)]
    base_part = jnp.dot(tokens, base_weight, preferred_element_type=f32)

    def columns(k):
        start = lax.rem(my_mp + k, parts) * local_columns
        return lax.dynamic_slice_in_dim(base_part, start, local_columns, axis=1)

    frozen = columns(0)
    for k in range(1, parts):
        frozen = frozen + shift(columns(k).astype(bf), "mp", parts, k).astype(f32)

    selected = select_up(ids_all, me, up_all, plane)
    slots = exchange(selected)
    rg_part = rank_grad_part(ids, slots, cotangent, owned)
    rg = (adapter_scale * mp_sum(rg_part)).astype(bf)
    rg_all = [rg] + [shift(rg, "g", plane, k) for k in range(1, plane)]

    part = rank_part(ids_row, me, table, tok_n)
    rank_parts = exchange(part)
    grad_table = down_terms(ids_all, me, rg_all, tok_n, adapters, rank)
    grad_n = lax.psum_scatter(grad_table, "z", scatter_dimension=0, tiled=True)
    chunks = grad_n.reshape(plane, owned, rank, narrow)
    grad_got = []
    for k in range(plane):
        part = lax.dynamic_index_in_dim(chunks, lax.rem(my_g + k, plane), 0, keepdims=False)
        grad_got.append(shift(part, "g", plane, k) if k else part)
    down_grad = down_gradient(me, grad_got)

    ranks = mp_sum(jnp.sum(rank_parts.astype(f32), axis=0)).astype(bf)

    through_n = through_down(ids_row, me, table, rg_all)
    through = [through_n[0]]
    through += [shift(through_n[k], "g", plane, plane - k) for k in range(1, plane)]
    input_grad = input_gradient(me, cots, base_weight, through)

    output, up_send = output_and_up(ids, ranks, slots, cotangent, frozen, owned)
    up_got = exchange(up_send)
    up_chunks = gather_up(ids_all, me, up_got, owned)
    up_got = exchange(up_chunks, "z")
    up_grad = jnp.sum(up_got.astype(f32), axis=0)
    return (output, input_grad, down_grad, up_grad)


def solution(mesh):
    fine = Mesh(mesh.devices.reshape(-1, PLANE, mesh.devices.shape[1]), ("z", "g", "mp"))
    dp = ("z", "g")
    return jax.shard_map(
        step,
        mesh=fine,
        in_specs=(
            P(dp, "mp"),
            P("mp", None),
            P(dp, None, "mp"),
            P(dp, None, "mp"),
            P(dp),
            P(dp, "mp"),
        ),
        out_specs=(P(dp, "mp"), P(dp, "mp"), P(dp, None, "mp"), P(dp, None, "mp")),
        check_vma=False,
    )
```

```python
import functools

import jax
import jax.numpy as jnp
from jax import lax
from jax.experimental import pallas as pl
from jax.experimental.pallas import tpu as pltpu
from jax.sharding import Mesh, PartitionSpec as P

adapter_scale = 2.0
PLANE = 8
QUAD = 4
f32, bf = jnp.float32, jnp.bfloat16

SMEM = functools.partial(pl.BlockSpec, memory_space=pltpu.SMEM)
VMEM = functools.partial(pl.BlockSpec, memory_space=pltpu.VMEM)


def diagonal(length, rank):
    rows = lax.broadcasted_iota(jnp.int32, (QUAD * length, QUAD * rank), 0) // length
    cols = lax.broadcasted_iota(jnp.int32, (QUAD * length, QUAD * rank), 1) // rank
    return rows == cols


def fold(product, mask, length):
    kept = jnp.where(mask, product, 0.0)
    total = kept[:length]
    for i in range(1, QUAD):
        total = total + kept[i * length : (i + 1) * length]
    return total


def spread(quad, mask):
    wide = jnp.concatenate([quad] * QUAD, axis=0)
    return jnp.where(mask, wide, jnp.zeros_like(wide))


def dot_nt(a, b):
    return lax.dot_general(a, b, (((1,), (1,)), ((), ())), preferred_element_type=f32)


def dot_nn(a, b):
    return lax.dot_general(a, b, (((1,), (0,)), ((), ())), preferred_element_type=f32)


def dot_tn(a, b):
    return lax.dot_general(a, b, (((0,), (0,)), ((), ())), preferred_element_type=f32)


HBM = functools.partial(pl.BlockSpec, memory_space=pl.ANY)


def stacked(count, like):
    return [pltpu.VMEM((count,) + like.shape, like.dtype), pltpu.SemaphoreType.DMA((count,))]


def load(refs, stack, sems):
    for k, ref in enumerate(refs):
        pltpu.make_async_copy(ref, stack.at[k], sems.at[k]).start()


def loaded(refs, stack, sems, k):
    pltpu.make_async_copy(refs[0], stack.at[k], sems.at[k]).wait()


def divide(x, n):
    return x >> (n.bit_length() - 1) if n & (n - 1) == 0 else lax.div(x, n)


def remainder(x, n):
    return x & (n - 1) if n & (n - 1) == 0 else lax.rem(x, n)


def back(me, k, size):
    return remainder(me - k + size, size)


def select_up(ids_all, me, gathered, plane):
    planes, owned, rank, cols = gathered.shape
    blocks = ids_all.shape[0] // plane

    def kernel(ids_ref, me_ref, all_ref, out_ref):
        my_g = me_ref[1]

        def step(b, carry):
            number = ids_ref[b]
            owner = divide(number, owned)

            @pl.when(remainder(owner, plane) == my_g)
            def _():
                z = divide(owner, plane)
                dest = back(my_g, divide(b, blocks), plane)
                out_ref[dest, z] = all_ref[z, remainder(number, owned)]

            return carry

        lax.fori_loop(0, plane * blocks, step, 0, unroll=2)

    return pl.pallas_call(
        kernel,
        in_specs=[SMEM(), SMEM(), VMEM()],
        out_specs=VMEM(),
        out_shape=jax.ShapeDtypeStruct((plane, planes, rank, cols), bf),
        name="select_up",
    )(ids_all, me, gathered)


def up_rows(ids_ref, slots_ref, q, owned, plane):
    rows = []
    for i in range(QUAD):
        owner = divide(ids_ref[q * QUAD + i], owned)
        rows.append(slots_ref[remainder(owner, plane), divide(owner, plane)])
    return jnp.concatenate(rows, axis=0)


def rank_grad_part(ids, slots, cot, owned):
    plane, _, rank, _ = slots.shape
    blocks = ids.shape[0]
    length = cot.shape[0] // blocks
    quads = blocks // QUAD
    span = QUAD * length

    def kernel(ids_ref, slots_ref, cot_ref, out_ref):
        mask = diagonal(length, rank)
        for q in range(quads):
            up = up_rows(ids_ref, slots_ref, q, owned, plane)
            out_ref[q] = fold(dot_nt(cot_ref[q * span : (q + 1) * span, :], up), mask, length)

    return pl.pallas_call(
        kernel,
        in_specs=[SMEM(), VMEM(), VMEM()],
        out_specs=VMEM(),
        out_shape=jax.ShapeDtypeStruct((quads, length, QUAD * rank), f32),
        name="rank_grad_part",
    )(ids, slots, cot)


def down_terms(ids_all, me, rg, tok, adapters, rank):
    plane = len(rg)
    quads, length = rg[0].shape[:2]
    span = QUAD * length
    blocks = quads * QUAD
    narrow = tok[0].shape[1]

    def kernel(ids_ref, me_ref, *refs):
        rgs, toks = refs[:plane], refs[plane : 2 * plane]
        out_ref, acc, rg_stack, rg_sems, tok_stack, tok_sems = refs[2 * plane :]
        mask = diagonal(length, rank)
        load(rgs, rg_stack, rg_sems)
        load(toks, tok_stack, tok_sems)

        def clear(c, carry):
            acc[pl.ds(c * 8, 8)] = jnp.zeros((8, rank, narrow), f32)
            return carry

        lax.fori_loop(0, adapters // 8, clear, 0)

        def step(k, carry):
            loaded(rgs, rg_stack, rg_sems, k)
            loaded(toks, tok_stack, tok_sems, k)
            for q in range(quads):
                wide = spread(rg_stack[k, q], mask)
                rows = tok_stack[k, q * span : (q + 1) * span, :]
                got = dot_tn(wide, rows) * (1.0 / length)
                for i in range(QUAD):
                    a = ids_ref[k * blocks + q * QUAD + i]
                    acc[a] = acc[a] + got[i * rank : (i + 1) * rank]
            return carry

        lax.fori_loop(0, plane, step, 0)

        def finish(c, carry):
            out_ref[pl.ds(c * 8, 8)] = acc[pl.ds(c * 8, 8)].astype(bf)
            return carry

        lax.fori_loop(0, adapters // 8, finish, 0)

    return pl.pallas_call(
        kernel,
        in_specs=[SMEM(), SMEM()] + [HBM()] * (2 * plane),
        out_specs=VMEM(),
        out_shape=jax.ShapeDtypeStruct((adapters, rank, narrow), bf),
        scratch_shapes=[pltpu.VMEM((adapters, rank, narrow), f32)]
        + stacked(plane, rg[0])
        + stacked(plane, tok[0]),
        name="down_terms",
    )(ids_all, me, *rg, *tok)


def table_rows(ids_ref, table_ref, first):
    return jnp.concatenate([table_ref[ids_ref[first + i]] for i in range(QUAD)], axis=0)


def rank_part(ids_all, me, table, tok):
    plane = len(tok)
    tokens, _ = tok[0].shape
    rank = table.shape[1]
    blocks = ids_all.shape[0] // plane
    length = tokens // blocks
    quads = blocks // QUAD
    span = QUAD * length

    def kernel(ids_ref, me_ref, table_ref, *refs):
        toks, (out_ref, stack, sems) = refs[:plane], refs[plane:]
        mask = diagonal(length, rank)
        load(toks, stack, sems)

        def step(k, carry):
            dest = back(me_ref[1], k, plane)
            loaded(toks, stack, sems, k)
            for q in range(quads):
                down = table_rows(ids_ref, table_ref, k * blocks + q * QUAD)
                got = dot_nt(stack[k, q * span : (q + 1) * span, :], down)
                out_ref[dest, q] = fold(got, mask, length).astype(bf)
            return carry

        lax.fori_loop(0, plane, step, 0)

    return pl.pallas_call(
        kernel,
        in_specs=[SMEM(), SMEM(), VMEM()] + [HBM()] * plane,
        out_specs=VMEM(),
        out_shape=jax.ShapeDtypeStruct((plane, quads, length, QUAD * rank), bf),
        scratch_shapes=stacked(plane, tok[0]),
        name="rank_part",
    )(ids_all, me, table, *tok)


def through_down(ids_all, me, table, rg):
    plane = len(rg)
    quads, length = rg[0].shape[:2]
    rank, narrow = table.shape[1:]
    span = QUAD * length
    blocks = quads * QUAD
    piece = jax.ShapeDtypeStruct((quads * span, narrow), bf)

    def kernel(ids_ref, me_ref, table_ref, *refs):
        rgs, outs = refs[:plane], refs[plane : 2 * plane]
        rg_stack, rg_sems, stack, sems = refs[2 * plane :]
        mask = diagonal(length, rank)
        load(rgs, rg_stack, rg_sems)

        def step(k, carry):
            loaded(rgs, rg_stack, rg_sems, k)
            for q in range(quads):
                down = table_rows(ids_ref, table_ref, k * blocks + q * QUAD)
                got = dot_nn(spread(rg_stack[k, q], mask), down)
                stack[k, q * span : (q + 1) * span, :] = got.astype(bf)
            return carry

        lax.fori_loop(0, plane, step, 0)
        for k in range(plane):
            pltpu.make_async_copy(stack.at[k], outs[k], sems.at[k]).start()
        for k in range(plane):
            pltpu.make_async_copy(stack.at[k], outs[k], sems.at[k]).wait()

    return pl.pallas_call(
        kernel,
        in_specs=[SMEM(), SMEM(), VMEM()] + [HBM()] * plane,
        out_specs=tuple([HBM()] * plane),
        out_shape=tuple([piece] * plane),
        scratch_shapes=stacked(plane, rg[0]) + stacked(plane, piece),
        name="through_down",
    )(ids_all, me, table, *rg)


def output_and_up(ids, ranks, slots, cot, base, owned):
    plane, _, rank, _ = slots.shape
    quads, length = ranks.shape[:2]
    span = QUAD * length

    def kernel(ids_ref, rank_ref, slots_ref, cot_ref, base_ref, out_ref, send_ref):
        mask = diagonal(length, rank)
        for q in range(quads):
            wide = spread(rank_ref[q], mask)
            up = up_rows(ids_ref, slots_ref, q, owned, plane)
            rows = slice(q * span, (q + 1) * span)
            out_ref[rows, :] = (base_ref[rows, :] + adapter_scale * dot_nn(wide, up)).astype(bf)
            got = (dot_tn(wide, cot_ref[rows, :]) * (adapter_scale / length)).astype(bf)
            for i in range(QUAD):
                owner = divide(ids_ref[q * QUAD + i], owned)
                send_ref[remainder(owner, plane), divide(owner, plane)] = got[i * rank : (i + 1) * rank]

    return pl.pallas_call(
        kernel,
        in_specs=[SMEM()] + [VMEM()] * 4,
        out_specs=(VMEM(), VMEM()),
        out_shape=(
            jax.ShapeDtypeStruct(cot.shape, bf),
            jax.ShapeDtypeStruct(slots.shape, bf),
        ),
        name="output_and_up",
    )(ids, ranks, slots, cot, base)


def gather_up(ids_all, me, got, owned):
    plane, planes, rank, cols = got.shape
    blocks = ids_all.shape[0] // plane

    def kernel(ids_ref, me_ref, got_ref, out_ref, acc):
        my_g = me_ref[1]
        acc[...] = jnp.zeros(acc.shape, f32)

        def step(b, carry):
            number = ids_ref[b]
            owner = divide(number, owned)

            @pl.when(remainder(owner, plane) == my_g)
            def _():
                z, local = divide(owner, plane), remainder(number, owned)
                acc[z, local] = acc[z, local] + got_ref[back(my_g, divide(b, blocks), plane), z].astype(f32)

            return carry

        lax.fori_loop(0, plane * blocks, step, 0, unroll=2)
        out_ref[...] = acc[...].astype(bf)

    shape = (planes, owned, rank, cols)
    return pl.pallas_call(
        kernel,
        in_specs=[SMEM(), SMEM(), VMEM()],
        out_specs=VMEM(),
        out_shape=jax.ShapeDtypeStruct(shape, bf),
        scratch_shapes=[pltpu.VMEM(shape, f32)],
        name="gather_up",
    )(ids_all, me, got)


def base_gradient(me, cots, weight):
    parts = len(cots)
    tokens, cols = cots[0].shape
    features = weight.shape[0]
    tile = 256

    def kernel(me_ref, *refs):
        w_ref, out_ref, whole = refs[parts:]

        @pl.when(pl.program_id(0) == 0)
        def _():
            for k in range(parts):
                first = pl.multiple_of(back(me_ref[2], k, parts) * cols, cols)
                whole[:, pl.ds(first, cols)] = refs[k][...]

        out_ref[...] = dot_nt(whole[...], w_ref[...])

    return pl.pallas_call(
        kernel,
        grid=(features // tile,),
        in_specs=[SMEM()]
        + [pl.BlockSpec((tokens, cols), lambda s: (0, 0))] * parts
        + [pl.BlockSpec((tile, parts * cols), lambda s: (s, 0))],
        out_specs=pl.BlockSpec((tokens, tile), lambda s: (0, s)),
        out_shape=jax.ShapeDtypeStruct((tokens, features), f32),
        scratch_shapes=[pltpu.VMEM((tokens, parts * cols), bf)],
        name="base_gradient",
    )(me, *cots, weight)


def input_gradient(me, base, through):
    plane = len(through)
    tokens, narrow = through[0].shape

    def kernel(me_ref, base_ref, *refs):
        out_ref = refs[plane]
        for k in range(plane):
            first = pl.multiple_of(remainder(me_ref[1] + k, plane) * narrow, narrow)
            cols = pl.ds(first, narrow)
            out_ref[:, cols] = (base_ref[:, cols] + refs[k][...].astype(f32)).astype(bf)

    return pl.pallas_call(
        kernel,
        in_specs=[SMEM()] + [VMEM()] * (plane + 1),
        out_specs=VMEM(),
        out_shape=jax.ShapeDtypeStruct((tokens, plane * narrow), bf),
        name="input_gradient",
    )(me, base, *through)


def pack_down(me, down, tile, plane):
    rows, width = down.shape
    narrow = width // plane
    piece = jax.ShapeDtypeStruct((rows + tile.shape[0], narrow), bf)

    def kernel(me_ref, down_ref, tile_ref, *outs):
        for k in range(plane):
            first = pl.multiple_of(lax.rem(me_ref[1] + k, plane) * narrow, narrow)
            outs[k][:rows, :] = down_ref[:, pl.ds(first, narrow)]
            outs[k][rows:, :] = tile_ref[...]

    return pl.pallas_call(
        kernel,
        in_specs=[SMEM(), VMEM(), VMEM()],
        out_specs=tuple([VMEM()] * plane),
        out_shape=tuple([piece] * plane),
        name="pack_down",
    )(me, down, tile)


def unpack_down(pieces, rows):
    plane = len(pieces)
    narrow = pieces[0].shape[1]

    def kernel(*refs):
        down_ref, ids_ref = refs[plane:]
        for k in range(plane):
            down_ref[k] = refs[k][:rows, :]
            ids_ref[k : k + 1, :] = refs[k][rows : rows + 1, :128].astype(f32).astype(jnp.int32)

    return pl.pallas_call(
        kernel,
        in_specs=[VMEM()] * plane,
        out_specs=(VMEM(), VMEM()),
        out_shape=(
            jax.ShapeDtypeStruct((plane, rows, narrow), bf),
            jax.ShapeDtypeStruct((plane, 128), jnp.int32),
        ),
        name="unpack_down",
    )(*pieces)


def down_gradient(me, pieces):
    plane = len(pieces)
    owned, rank, narrow = pieces[0].shape

    def kernel(me_ref, *refs):
        out_ref = refs[plane]
        for k in range(plane):
            first = pl.multiple_of(back(me_ref[1], k, plane) * narrow, narrow)
            out_ref[:, :, pl.ds(first, narrow)] = refs[k][...].astype(f32)

    return pl.pallas_call(
        kernel,
        in_specs=[SMEM()] + [VMEM()] * plane,
        out_specs=VMEM(),
        out_shape=jax.ShapeDtypeStruct((owned, rank, plane * narrow), f32),
        name="down_gradient",
    )(me, *pieces)


def shift(x, axis, size, k):
    return lax.ppermute(x, axis, [(i, (i + k) % size) for i in range(size)])


def step(tokens, base_weight, adapter_down, adapter_up, block_adapter, cotangent):
    blocks = block_adapter.shape[0]
    owned, rank, width_local = adapter_down.shape
    _, local_columns = cotangent.shape
    planes, plane, parts = lax.axis_size("z"), lax.axis_size("g"), lax.axis_size("mp")
    my_mp = lax.axis_index("mp")
    my_g = lax.axis_index("g")
    me = jnp.stack([lax.axis_index("z"), my_g, my_mp]).astype(jnp.int32)
    adapters = planes * plane * owned
    narrow = width_local // plane

    def exchange(x, axis="g"):
        return lax.all_to_all(x, axis, split_axis=0, concat_axis=0, tiled=True)

    def mp_sum(x):
        total = x
        for k in range(1, parts):
            total = total + shift(x, "mp", parts, k)
        return total

    ids = block_adapter
    up_all = exchange(jnp.broadcast_to(adapter_up[None], (planes,) + adapter_up.shape), "z")
    rows = owned * rank
    tile = jnp.pad(ids.astype(bf)[None], ((0, 15), (0, narrow - blocks)))
    packed = pack_down(me, adapter_down.reshape(rows, width_local), tile, plane)
    got = [packed[0]] + [shift(packed[k], "g", plane, k) for k in range(1, plane)]
    down_n, ids_rows = unpack_down(got, rows)
    table = lax.all_gather(down_n.reshape(-1, rank, narrow), "z", axis=0, tiled=True)
    ids_all = ids_rows[:, :blocks].reshape(-1)
    owner = ids_all // owned
    steps = lax.rem(my_g - owner % plane + plane, plane)
    ids_row = (owner // plane * plane + steps) * owned + ids_all % owned
    tok_n = []
    for k in range(plane):
        first = lax.rem(my_g + k, plane) * narrow
        part = lax.dynamic_slice_in_dim(tokens, first, narrow, axis=1)
        tok_n.append(shift(part, "g", plane, k) if k else part)
    cots = [cotangent] + [shift(cotangent, "mp", parts, k) for k in range(1, parts)]
    base_part = jnp.dot(tokens, base_weight, preferred_element_type=f32)

    def columns(k):
        start = lax.rem(my_mp + k, parts) * local_columns
        return lax.dynamic_slice_in_dim(base_part, start, local_columns, axis=1)

    frozen = columns(0)
    for k in range(1, parts):
        frozen = frozen + shift(columns(k).astype(bf), "mp", parts, k).astype(f32)

    selected = select_up(ids_all, me, up_all, plane)
    slots = exchange(selected)
    rg_part = rank_grad_part(ids, slots, cotangent, owned)
    rg = (adapter_scale * mp_sum(rg_part)).astype(bf)
    rg_all = [rg] + [shift(rg, "g", plane, k) for k in range(1, plane)]

    part = rank_part(ids_row, me, table, tok_n)
    rank_parts = exchange(part)
    grad_table = down_terms(ids_all, me, rg_all, tok_n, adapters, rank)
    grad_n = lax.psum_scatter(grad_table, "z", scatter_dimension=0, tiled=True)
    chunks = grad_n.reshape(plane, owned, rank, narrow)
    grad_got = []
    for k in range(plane):
        part = lax.dynamic_index_in_dim(chunks, lax.rem(my_g + k, plane), 0, keepdims=False)
        grad_got.append(shift(part, "g", plane, k) if k else part)
    down_grad = down_gradient(me, grad_got)

    ranks = mp_sum(jnp.sum(rank_parts.astype(f32), axis=0)).astype(bf)

    through_n = through_down(ids_row, me, table, rg_all)
    through = [through_n[0]]
    for k in range(1, plane):
        through.append(shift(through_n[k], "g", plane, plane - k))
    base_grad = base_gradient(me, cots, base_weight)
    input_grad = input_gradient(me, base_grad, through)

    output, up_send = output_and_up(ids, ranks, slots, cotangent, frozen, owned)
    up_got = exchange(up_send)
    up_chunks = gather_up(ids_all, me, up_got, owned)
    up_got = exchange(up_chunks, "z")
    up_grad = jnp.sum(up_got.astype(f32), axis=0)
    return (output, input_grad, down_grad, up_grad)


def solution(mesh):
    fine = Mesh(mesh.devices.reshape(-1, PLANE, mesh.devices.shape[1]), ("z", "g", "mp"))
    dp = ("z", "g")
    return jax.shard_map(
        step,
        mesh=fine,
        in_specs=(
            P(dp, "mp"),
            P("mp", None),
            P(dp, None, "mp"),
            P(dp, None, "mp"),
            P(dp),
            P(dp, "mp"),
        ),
        out_specs=(P(dp, "mp"), P(dp, "mp"), P(dp, None, "mp"), P(dp, None, "mp")),
        check_vma=False,
    )
```
